32 devices in a mesh: grp: 2 (over y), dp: 4 (over z), tensor: 4 (over x, core).
Axes of the slice: x: 2, y: 2, z: 4, core: 2. Of those that a mesh axis runs over, the one named last changes fastest.
Arguments:
- x_train: bfloat16 [1024, 28672], P(('grp', 'dp'), 'tensor'), parts along dimension 0, may hold values from -6 to 6
- gout_train: bfloat16 [1024, 8192], P(('grp', 'dp'), 'tensor'), parts along dimension 0, may hold values from -6 to 6
- x_query: bfloat16 [256, 28672], P(('grp', 'dp'), 'tensor'), parts along dimension 0, may hold values from -6 to 6
- gout_query: bfloat16 [256, 8192], P(('grp', 'dp'), 'tensor'), parts along dimension 0, may hold values from -6 to 6
- proj_in: bfloat16 [28672, 64], P('tensor'), may hold values from -0.03125 to 0.03125
- proj_out: bfloat16 [8192, 32], P('tensor'), may hold values from -0.0625 to 0.0625
- train_lengths: int32 [64], P(('grp', 'dp')), parts along dimension 0, may hold values from 1 to 16, 384 in all
- query_lengths: int32 [16], P(('grp', 'dp')), parts along dimension 0, may hold values from 1 to 16, 96 in all
- damping: int32 [1], replicated, may hold values from 3 to 10
Outputs:
- train_grads: bfloat16 [64, 2048], P(('grp', 'dp'), 'tensor'), parts along dimension 0
- query_grads: bfloat16 [16, 2048], P(('grp', 'dp'), 'tensor'), parts along dimension 0
- scores: float32 [64, 8], P(('grp', 'dp')), parts along dimension 0
The draws below stay inside these ranges and needn't reach their ends.
There are 2 independent parts, one for each index of `grp`. The reference program is written for one: setup_inputs(seed, part) draws one part's arguments, and reference() takes and returns one part's arrays. A program takes and returns all parts, laid end to end along the dimension named above; an argument that names none is the same for every part. Nothing has to cross between parts.
Inputs may be any that keep to these rules, and one draw needn't show every extreme that they name: `train_lengths`: each example has 1 to 16 valid tokens, the first ones of its slots; within each part (one corpus shard of 32 examples) the train lengths sum to 384 and some train example of that part has 16; the whole array, all parts end to end, sums to that amount times the number of parts. `query_lengths`: within each part (one corpus shard of 8 examples) the query lengths sum to 96 and some query example of that part has 16; the whole array sums to that amount times the number of parts.
All inputs are finite; a program needn't handle non-finite values.
Results may differ from the reference program's by a relative error of at most 0.0038.
Values may be sent and summed in bfloat16 or wider, within the bound.
A program may use at most 64 MiB of HBM per device.

```python
import math
import jax
import jax.numpy as jnp
import numpy as np
from jax import lax

DIN = 28672
DOUT = 8192
RIN = 64
ROUT = 32
L = 16
N_TR = 32
N_Q = 8


ladder_weights = (20, 13, 10, 8, 7, 6, 5, 5, 4, 4, 4, 3, 3, 3, 3, 3, 2, 2, 2, 2, 2, 2, 2, 2)


def shared_signs(key, shared_code, directions, columns):
    random_bits = jax.random.randint(jax.random.fold_in(key, shared_code), (directions, columns), 0, 2)
    return (2 * random_bits - 1).astype(jnp.float32)


def token_field(key, salt_code, shared_code, row_total, columns, directions):
    signs = shared_signs(key, shared_code, directions, columns)
    levels = jax.random.randint(jax.random.fold_in(key, salt_code), (row_total, directions), -2, 3)
    ladder = jnp.array(ladder_weights[:directions], dtype=jnp.int32)
    coded = (levels * ladder[None, :]).astype(jnp.float32)
    shared = jnp.zeros((row_total, columns), jnp.float32)
    for direction in range(directions):
        shared = shared + coded[:, direction:direction + 1] * signs[direction][None, :]
    shared = shared * 0.03125
    noise_key = jax.random.fold_in(key, salt_code + 1000)
    noise = 0.5 * jax.random.normal(noise_key, (row_total, columns), jnp.float32)
    field = noise + shared
    return jnp.clip(field, -6.0, 6.0).astype(jnp.bfloat16)


def draw_x_train(key, part):
    return token_field(key, 31, 11, N_TR * L, DIN, 24)


def draw_gout_train(key, part):
    return token_field(key, 41, 12, N_TR * L, DOUT, 16)


def draw_x_query(key, part):
    return token_field(key, 51, 11, N_Q * L, DIN, 24)


def draw_gout_query(key, part):
    return token_field(key, 61, 12, N_Q * L, DOUT, 16)


def level_of(own_key, dims, pieces, least, top_value):
    def one(axis_at, shards_of):
        steps = jax.random.uniform(jax.random.fold_in(jax.random.fold_in(own_key, 6), axis_at), (shards_of,), jnp.float32, least / len(pieces), top_value / len(pieces))
        return jnp.repeat(jnp.exp(steps), dims[axis_at] // shards_of).reshape((-1,) + (1,) * (len(dims) - axis_at - 1))

    gain = one(*pieces[0])
    for cut in pieces[1:]:
        gain = gain * one(*cut)
    return gain


def length_profile(amount, total, reach, skew):
    portions = [(1 << 20) // math.isqrt(standing ** skew) + 1 for standing in range(2, amount + 1)]
    rest, given = total - reach - (amount - 1), [1] * (amount - 1)
    while rest > 0:
        candidates = [i for i in range(amount - 1) if given[i] < reach]
        mass, left = sum([portions[i] for i in candidates]), rest
        for i in candidates:
            addition = min(reach - given[i], max(1, left * portions[i] // mass), rest)
            given[i] = given[i] + addition
            rest = rest - addition
    return np.array([reach] + given)


def ragged_sizes(key, number_of, total, reach, slope):
    if number_of == 2:
        one = jax.random.randint(key, (), max(1, total - reach), min(reach, total - 1) + 1)
        return jnp.stack([one, total - one])
    tallies = jnp.asarray(length_profile(number_of, total, reach, slope), jnp.int32)
    twos = (number_of - 1) // 2
    source_of, receiver = tallies[1:1 + 2 * twos:2], tallies[2:2 + 2 * twos:2]
    slack = jnp.minimum(source_of - 1, reach - receiver)
    shifted = jax.random.randint(jax.random.fold_in(key, 1), (twos,), 0, 1 << 20) % (slack + 1)
    tallies = tallies.at[1:1 + 2 * twos:2].set(source_of - shifted).at[2:2 + 2 * twos:2].set(receiver + shifted)
    return tallies[jax.random.permutation(jax.random.fold_in(key, 2), number_of)]


def normal_values(stream_key, dims, width, limit, shards=(), held_as=jnp.bfloat16):
    entries = jax.random.normal(stream_key, dims, jnp.float32) * width
    if len(shards) > 0:
        entries = level_of(stream_key, dims, shards, -0.22, 0.18) * entries
    return jnp.clip(entries, min=-limit, max=limit).astype(held_as)


def setup_inputs(seed: int = 0, part: int = 0) -> dict:
    arg_keys = jax.random.split(jax.random.key(seed), 10)
    part_splits = jax.random.split(jax.random.fold_in(arg_keys[9], part), 10)
    return {
        "x_train": draw_x_train(jax.random.fold_in(jax.random.fold_in(arg_keys[9], part), 71), part),
        "gout_train": draw_gout_train(jax.random.fold_in(jax.random.fold_in(arg_keys[9], part), 71), part),
        "x_query": draw_x_query(jax.random.fold_in(jax.random.fold_in(arg_keys[9], part), 71), part),
        "gout_query": draw_gout_query(jax.random.fold_in(jax.random.fold_in(arg_keys[9], part), 71), part),
        "proj_in": normal_values(arg_keys[4], (DIN, RIN), DIN ** -0.5, 0.03125, ((0, 4),)),
        "proj_out": normal_values(arg_keys[5], (DOUT, ROUT), DOUT ** -0.5, 0.0625, ((0, 4),)),
        "train_lengths": ragged_sizes(part_splits[6], N_TR, N_TR * L * 3 // 4, L, 0).astype(jnp.int32),
        "query_lengths": ragged_sizes(part_splits[7], N_Q, N_Q * L * 3 // 4, L, 0).astype(jnp.int32),
        "damping": jax.random.randint(arg_keys[8], (1,), 3, 11).astype(jnp.int32),
    }


def example_grads(tokens, cotangents, proj_in, proj_out, lengths):
    inner = jnp.dot(tokens.astype(jnp.float32), proj_in.astype(jnp.float32), preferred_element_type=jnp.float32)
    outer = jnp.dot(cotangents.astype(jnp.float32), proj_out.astype(jnp.float32), preferred_element_type=jnp.float32)
    count = lengths.shape[0]
    inner = inner.reshape(count, L, RIN)
    outer = outer.reshape(count, L, ROUT)
    valid = (jnp.arange(L, dtype=jnp.int32)[None, :] < lengths[:, None]).astype(jnp.float32)
    weight = valid / lengths[:, None].astype(jnp.float32)
    summed = jnp.einsum('eti,eto->eio', inner * weight[:, :, None], outer, precision=lax.Precision.HIGHEST)
    return summed.reshape(count, RIN * ROUT).astype(jnp.bfloat16)

def reference(x_train, gout_train, x_query, gout_query, proj_in, proj_out, train_lengths, query_lengths, damping):
    train_grads = example_grads(x_train, gout_train, proj_in, proj_out, train_lengths)
    query_grads = example_grads(x_query, gout_query, proj_in, proj_out, query_lengths)
    kernel = jnp.dot(train_grads.astype(jnp.float32), train_grads.T.astype(jnp.float32), preferred_element_type=jnp.float32)
    cross = jnp.dot(train_grads.astype(jnp.float32), query_grads.T.astype(jnp.float32), preferred_element_type=jnp.float32)
    widened = train_grads.astype(jnp.float32)
    trace = jnp.sum(widened * widened)
    ridge = damping[0].astype(jnp.float32) / 10.0 * trace / N_TR
    system = kernel + ridge * jnp.eye(N_TR, dtype=jnp.float32)
    factor = jnp.linalg.cholesky(system)
    solved = jax.scipy.linalg.cho_solve((factor, True), cross)
    return (train_grads, query_grads, solved * N_TR)
```

```python
import functools

import jax
import jax.numpy as jnp
from jax import lax
from jax.experimental import pallas as pl
from jax.experimental.pallas import tpu as pltpu
from jax.sharding import PartitionSpec as P


def weighted_grads(inner, outer, lengths):
    count = lengths.shape[0]
    slots = inner.shape[0] // count
    inner = inner.reshape(count, slots, inner.shape[1])
    outer = outer.reshape(count, slots, outer.shape[1])
    valid = (lax.broadcasted_iota(jnp.int32, (count, slots), 1) < lengths[:, None]).astype(
        jnp.float32
    )
    weight = valid / lengths[:, None].astype(jnp.float32)
    summed = jnp.einsum(
        "eti,eto->eio", inner * weight[:, :, None], outer, precision=lax.Precision.HIGHEST
    )
    return summed.reshape(count, -1).astype(jnp.bfloat16)


def kernel_scores(kernel, cross, scale_code, total_train, first, local_train):
    trace = jnp.trace(kernel)
    ridge = scale_code * trace / total_train
    system = kernel + ridge * jnp.eye(total_train, dtype=jnp.float32)
    factor = jnp.linalg.cholesky(system)
    solved = jax.scipy.linalg.cho_solve((factor, True), cross)
    picked = lax.dynamic_slice_in_dim(solved, first, local_train, 0)
    return picked * total_train


MESH = pl.DeviceIdType.MESH
CHUNKS = 4
ROWS = 16


def fits_fused(x_train, x_query, proj_in, proj_out, train_lengths, query_lengths):
    train_count, query_count = train_lengths.shape[0], query_lengths.shape[0]
    tensor, dp = lax.axis_size("tensor"), lax.axis_size("dp")
    return (
        tensor > 1
        and dp > 1
        and train_count == 8
        and query_count <= 8
        and x_train.shape[0] == 128
        and x_query.shape[0] <= 128
        and x_query.shape[0] % 16 == 0
        and x_query.shape[0] // query_count == 16
        and proj_in.shape[0] % (128 * CHUNKS) == 0
        and proj_in.shape[1] % (8 * tensor) == 0
        and proj_out.shape[1] % 8 == 0
        and dp * ROWS <= 128
    )


def eliminate(system, columns):
    count = len(columns)
    row_id = lax.broadcasted_iota(jnp.int32, system.shape, 0)
    for k in range(count):
        c = columns[k]
        column = system[:, c : c + 1]
        scaled = system[k : k + 1, :] / system[k : k + 1, c : c + 1]
        system = jnp.where(row_id == k, scaled, system - column * scaled)
    return system


def fused_kernel(
    tensor,
    dp,
    query_count,
    xt,
    gt,
    xq,
    gq,
    pin,
    pout,
    tlen,
    qlen,
    damp,
    out_train,
    out_query,
    out_scores,
    xv,
    gv,
    piv,
    pov,
    tls,
    qls,
    dms,
    acc,
    got_inner,
    got_outer,
    grads,
    grams,
    solved,
    load_sem,
    small_sem,
    send_outer,
    recv_outer,
    send_inner,
    recv_inner,
    send_grads,
    recv_grads,
    send_gram,
    recv_gram,
):
    me_t, me_d = lax.axis_index("tensor"), lax.axis_index("dp")
    peers_t = [lax.rem(me_t + k, tensor) for k in range(1, tensor)]
    peers_d = [lax.rem(me_d + k, dp) for k in range(1, dp)]
    rows_t, rows_q = xt.shape[0], xq.shape[0]
    rank_in, rank_out = pin.shape[0], pout.shape[0]
    share = rank_in // tensor
    width = pin.shape[1] // CHUNKS
    tokens = rows_t + rows_q

    loads = [
        pltpu.make_async_copy(gt, gv.at[pl.ds(0, rows_t), :], load_sem.at[0]),
        pltpu.make_async_copy(gq, gv.at[pl.ds(rows_t, rows_q), :], load_sem.at[1]),
        pltpu.make_async_copy(pout, pov, load_sem.at[2]),
    ]
    chunk_loads = []
    for chunk in range(CHUNKS):
        at = pl.ds(chunk * width, width)
        base = 3 + 3 * chunk
        chunk_loads.append(
            [
                pltpu.make_async_copy(xt.at[:, at], xv.at[pl.ds(0, rows_t), at], load_sem.at[base]),
                pltpu.make_async_copy(xq.at[:, at], xv.at[pl.ds(rows_t, rows_q), at], load_sem.at[base + 1]),
                pltpu.make_async_copy(pin.at[:, at], piv.at[:, at], load_sem.at[base + 2]),
            ]
        )
    small = [
        pltpu.make_async_copy(tlen, tls, small_sem.at[0]),
        pltpu.make_async_copy(qlen, qls, small_sem.at[1]),
        pltpu.make_async_copy(damp, dms, small_sem.at[2]),
    ]
    for copy in loads:
        copy.start()
    for group in chunk_loads:
        for copy in group:
            copy.start()
    for copy in small:
        copy.start()

    barrier = pltpu.get_barrier_semaphore()
    for peer in peers_t:
        pl.semaphore_signal(barrier, inc=1, device_id={"tensor": peer}, device_id_type=MESH)
    for peer in peers_d:
        pl.semaphore_signal(barrier, inc=1, device_id={"dp": peer}, device_id_type=MESH)

    acc[:, 128:] = jnp.zeros((acc.shape[0], acc.shape[1] - 128), jnp.float32)
    contract = (((1,), (1,)), ((), ()))

    for copy in loads:
        copy.wait()
    outer = lax.dot_general(pov[...], gv[...], contract, preferred_element_type=jnp.float32)
    acc[pl.ds(rank_in, rank_out), pl.ds(0, tokens)] = outer

    pl.semaphore_wait(barrier, tensor - 1 + dp - 1)
    outer_copies = []
    for k, peer in enumerate(peers_t):
        copy = pltpu.make_async_remote_copy(
            src_ref=acc.at[pl.ds(rank_in, rank_out), :],
            dst_ref=got_outer.at[k],
            send_sem=send_outer.at[k],
            recv_sem=recv_outer.at[k],
            device_id={"tensor": peer},
            device_id_type=MESH,
        )
        copy.start()
        outer_copies.append(copy)

    inner = None
    for chunk in range(CHUNKS):
        for copy in chunk_loads[chunk]:
            copy.wait()
        at = pl.ds(chunk * width, width)
        part = lax.dot_general(piv[:, at], xv[:, at], contract, preferred_element_type=jnp.float32)
        inner = part if inner is None else inner + part
    acc[pl.ds(0, rank_in), pl.ds(0, tokens)] = inner

    inner_copies = []
    for k, peer in enumerate(peers_t):
        copy = pltpu.make_async_remote_copy(
            src_ref=acc.at[pl.ds(pl.multiple_of(peer * share, share), share), :],
            dst_ref=got_inner.at[k],
            send_sem=send_inner.at[k],
            recv_sem=recv_inner.at[k],
            device_id={"tensor": peer},
            device_id_type=MESH,
        )
        copy.start()
        inner_copies.append(copy)

    for copy in small:
        copy.wait()
    row_id = lax.broadcasted_iota(jnp.int32, (ROWS, 128), 0)
    lane_id = lax.broadcasted_iota(jnp.int32, (ROWS, 128), 1)
    lengths = jnp.ones((ROWS, 128), jnp.int32)
    for e in range(8):
        lengths = jnp.where(row_id == e, tls[e], lengths)
    for e in range(query_count):
        lengths = jnp.where(row_id == 8 + e, qls[e], lengths)
    slot, example = lane_id % 16, lane_id // 16
    train_mask = (row_id < 8) & (example == row_id) & (slot < lengths)
    query_mask = (row_id >= 8) & (row_id < 8 + query_count) & (example == row_id - 8) & (slot < lengths)
    train_mask = jnp.where(train_mask, 1.0, 0.0).astype(jnp.bfloat16)
    query_mask = jnp.where(query_mask, 1.0, 0.0).astype(jnp.bfloat16)
    masks = jnp.concatenate([train_mask, query_mask, train_mask, query_mask], axis=1)
    real_lengths = lengths[:, :1].astype(jnp.float32)
    scale_code = dms[0].astype(jnp.float32) / 10.0

    outer_sum = acc[pl.ds(rank_in, rank_out), :]
    for k, copy in enumerate(outer_copies):
        copy.wait_recv()
        outer_sum = outer_sum + got_outer[k]
    inner_sum = acc[pl.ds(pl.multiple_of(me_t * share, share), share), :]
    for k, copy in enumerate(inner_copies):
        copy.wait_recv()
        inner_sum = inner_sum + got_inner[k]

    products = jnp.concatenate([inner_sum[i : i + 1, :] * outer_sum for i in range(share)], axis=0)
    high = products.astype(jnp.bfloat16)
    low = (products - high.astype(jnp.float32)).astype(jnp.bfloat16)
    summed = lax.dot_general(
        masks, jnp.concatenate([high, low], axis=1), contract, preferred_element_type=jnp.float32
    )
    mine = (summed / real_lengths).astype(jnp.bfloat16)
    grads[me_d] = mine

    grad_copies = []
    for k, peer in enumerate(peers_d):
        copy = pltpu.make_async_remote_copy(
            src_ref=grads.at[me_d],
            dst_ref=grads.at[me_d],
            send_sem=send_grads.at[k],
            recv_sem=recv_grads.at[k],
            device_id={"dp": peer},
            device_id_type=MESH,
        )
        copy.start()
        grad_copies.append(copy)
    out_train[...] = mine[:8, :]
    out_query[...] = mine[8 : 8 + query_count, :]
    for copy in grad_copies:
        copy.wait_recv()

    everyone = grads[...].reshape(dp * ROWS, mine.shape[1])
    gram = lax.dot_general(everyone, everyone, contract, preferred_element_type=jnp.float32)
    gram = jnp.concatenate([gram[d * ROWS : d * ROWS + 8, :] for d in range(dp)], axis=0)
    grams[me_t, :, pl.ds(0, dp * ROWS)] = gram
    gram_copies = []
    for k, peer in enumerate(peers_t):
        copy = pltpu.make_async_remote_copy(
            src_ref=grams.at[me_t],
            dst_ref=grams.at[me_t],
            send_sem=send_gram.at[k],
            recv_sem=recv_gram.at[k],
            device_id={"tensor": peer},
            device_id_type=MESH,
        )
        copy.start()
        gram_copies.append(copy)
    for copy in gram_copies:
        copy.wait_recv()
    whole = grams[0][:, : dp * ROWS]
    for t in range(1, tensor):
        whole = whole + grams[t][:, : dp * ROWS]

    total = dp * 8
    row = lax.broadcasted_iota(jnp.int32, whole.shape, 0)
    lane = lax.broadcasted_iota(jnp.int32, whole.shape, 1)
    diagonal = lane == (row // 8) * ROWS + row % 8
    trace = jnp.sum(jnp.where(diagonal, whole, 0.0), axis=(0, 1), keepdims=True)
    ridge = scale_code * trace / total
    system = jnp.where(diagonal, whole + ridge, whole)
    columns = [(e // 8) * ROWS + e % 8 for e in range(total)]
    solved[...] = eliminate(system, columns)
    picked = solved[pl.ds(pl.multiple_of(me_d * 8, 8), 8), :] * total
    for d in range(dp):
        out_scores[:, d * query_count : (d + 1) * query_count] = picked[
            :, d * ROWS + 8 : d * ROWS + 8 + query_count
        ]

    for copy in outer_copies + inner_copies + grad_copies + gram_copies:
        copy.wait_send()


def fused_call(x_train, gout_train, x_query, gout_query, proj_in, proj_out, train_lengths, query_lengths, damping):
    tensor, dp = lax.axis_size("tensor"), lax.axis_size("dp")
    query_count = query_lengths.shape[0]
    rank_in, rank_out = proj_in.shape[1], proj_out.shape[1]
    depth_in, depth_out = proj_in.shape[0], proj_out.shape[0]
    tokens = x_train.shape[0] + x_query.shape[0]
    share = rank_in // tensor
    features = share * rank_out
    anywhere = pl.BlockSpec(memory_space=pl.ANY)
    vmem = pl.BlockSpec(memory_space=pltpu.VMEM)
    dma = pltpu.SemaphoreType.DMA
    return pl.pallas_call(
        functools.partial(fused_kernel, tensor, dp, query_count),
        out_shape=(
            jax.ShapeDtypeStruct((8, features), jnp.bfloat16),
            jax.ShapeDtypeStruct((query_count, features), jnp.bfloat16),
            jax.ShapeDtypeStruct((8, dp * query_count), jnp.float32),
        ),
        in_specs=[anywhere] * 9,
        out_specs=(vmem, vmem, vmem),
        scratch_shapes=[
            pltpu.VMEM((tokens, depth_in), jnp.bfloat16),
            pltpu.VMEM((tokens, depth_out), jnp.bfloat16),
            pltpu.VMEM((rank_in, depth_in), jnp.bfloat16),
            pltpu.VMEM((rank_out, depth_out), jnp.bfloat16),
            pltpu.SMEM(train_lengths.shape, jnp.int32),
            pltpu.SMEM(query_lengths.shape, jnp.int32),
            pltpu.SMEM(damping.shape, jnp.int32),
            pltpu.VMEM((rank_in + rank_out, 256), jnp.float32),
            pltpu.VMEM((tensor - 1, share, 256), jnp.float32),
            pltpu.VMEM((tensor - 1, rank_out, 256), jnp.float32),
            pltpu.VMEM((dp, ROWS, features), jnp.bfloat16),
            pltpu.VMEM((tensor, dp * 8, 128), jnp.float32),
            pltpu.VMEM((dp * 8, dp * ROWS), jnp.float32),
            dma((3 + 3 * CHUNKS,)),
            dma((3,)),
            dma((tensor - 1,)),
            dma((tensor - 1,)),
            dma((tensor - 1,)),
            dma((tensor - 1,)),
            dma((dp - 1,)),
            dma((dp - 1,)),
            dma((tensor - 1,)),
            dma((tensor - 1,)),
        ],
        compiler_params=pltpu.CompilerParams(
            collective_id=0, has_side_effects=True, vmem_limit_bytes=48 << 20
        ),
        name="fused_scores",
    )(
        x_train,
        gout_train,
        x_query,
        gout_query,
        proj_in.T,
        proj_out.T,
        train_lengths,
        query_lengths,
        damping,
    )


def shards(
    x_train,
    gout_train,
    x_query,
    gout_query,
    proj_in,
    proj_out,
    train_lengths,
    query_lengths,
    damping,
):
    local_train = train_lengths.shape[0]
    total_train = local_train * lax.axis_size("dp")
    if fits_fused(x_train, x_query, proj_in, proj_out, train_lengths, query_lengths):
        return fused_call(
            x_train, gout_train, x_query, gout_query, proj_in, proj_out, train_lengths, query_lengths, damping
        )
    first = lax.axis_index("dp") * local_train
    scale_code = damping[0].astype(jnp.float32) / 10.0
    train_inner = jnp.dot(x_train, proj_in, preferred_element_type=jnp.float32)
    query_inner = jnp.dot(x_query, proj_in, preferred_element_type=jnp.float32)
    train_outer = jnp.dot(gout_train, proj_out, preferred_element_type=jnp.float32)
    query_outer = jnp.dot(gout_query, proj_out, preferred_element_type=jnp.float32)
    summed = lax.psum((train_inner, query_inner, train_outer, query_outer), "tensor")
    train_full = weighted_grads(summed[0], summed[2], train_lengths)
    query_full = weighted_grads(summed[1], summed[3], query_lengths)
    share = train_full.shape[1] // lax.axis_size("tensor")
    offset = lax.axis_index("tensor") * share
    train_grads = lax.dynamic_slice_in_dim(train_full, offset, share, 1)
    query_grads = lax.dynamic_slice_in_dim(query_full, offset, share, 1)
    all_train, all_query = (
        lax.all_gather(train_full, "dp", axis=0, tiled=True),
        lax.all_gather(query_full, "dp", axis=0, tiled=True),
    )
    kernel = jnp.dot(all_train, all_train.T, preferred_element_type=jnp.float32)
    cross = jnp.dot(all_train, all_query.T, preferred_element_type=jnp.float32)
    scores = kernel_scores(kernel, cross, scale_code, total_train, first, local_train)
    return (train_grads, query_grads, scores)


def solution(mesh):
    placed = (
        P(("grp", "dp"), "tensor"),
        P(("grp", "dp"), "tensor"),
        P(("grp", "dp"), "tensor"),
        P(("grp", "dp"), "tensor"),
        P("tensor", None),
        P("tensor", None),
        P(("grp", "dp")),
        P(("grp", "dp")),
        P(),
    )
    return jax.shard_map(
        shards,
        mesh=mesh,
        in_specs=placed,
        out_specs=(P(("grp", "dp"), "tensor"), P(("grp", "dp"), "tensor"), P(("grp", "dp"), None)),
        check_vma=False,
    )
```

```python
import functools

import jax
import jax.numpy as jnp
from jax import lax
from jax.experimental import pallas as pl
from jax.experimental.pallas import tpu as pltpu
from jax.sharding import PartitionSpec as P


def weighted_grads(inner, outer, lengths):
    count = lengths.shape[0]
    slots = inner.shape[0] // count
    inner = inner.reshape(count, slots, inner.shape[1])
    outer = outer.reshape(count, slots, outer.shape[1])
    valid = (lax.broadcasted_iota(jnp.int32, (count, slots), 1) < lengths[:, None]).astype(
        jnp.float32
    )
    weight = valid / lengths[:, None].astype(jnp.float32)
    summed = jnp.einsum(
        "eti,eto->eio", inner * weight[:, :, None], outer, precision=lax.Precision.HIGHEST
    )
    return summed.reshape(count, -1).astype(jnp.bfloat16)


def kernel_scores(kernel, cross, scale_code, total_train, first, local_train):
    trace = jnp.trace(kernel)
    ridge = scale_code * trace / total_train
    system = kernel + ridge * jnp.eye(total_train, dtype=jnp.float32)
    factor = jnp.linalg.cholesky(system)
    solved = jax.scipy.linalg.cho_solve((factor, True), cross)
    picked = lax.dynamic_slice_in_dim(solved, first, local_train, 0)
    return picked * total_train


MESH = pl.DeviceIdType.MESH
CHUNKS = 4
ROWS = 16


def fits_fused(x_train, x_query, proj_in, proj_out, train_lengths, query_lengths):
    train_count, query_count = train_lengths.shape[0], query_lengths.shape[0]
    tensor, dp = lax.axis_size("tensor"), lax.axis_size("dp")
    return (
        tensor > 1
        and dp > 1
        and train_count == 8
        and query_count <= 8
        and x_train.shape[0] == 128
        and x_query.shape[0] <= 128
        and x_query.shape[0] % 16 == 0
        and x_query.shape[0] // query_count == 16
        and proj_in.shape[0] % (128 * CHUNKS) == 0
        and proj_in.shape[1] % (8 * tensor) == 0
        and proj_out.shape[1] % 8 == 0
        and dp * ROWS <= 128
    )


def eliminate(system, columns):
    count = len(columns)
    row_id = lax.broadcasted_iota(jnp.int32, system.shape, 0)
    for k in range(count):
        c = columns[k]
        column = system[:, c : c + 1]
        scaled = system[k : k + 1, :] / system[k : k + 1, c : c + 1]
        system = jnp.where(row_id == k, scaled, system - column * scaled)
    return system


def fused_kernel(
    tensor,
    dp,
    query_count,
    xt,
    gt,
    xq,
    gq,
    pin,
    pout,
    tlen,
    qlen,
    damp,
    out_train,
    out_query,
    out_scores,
    xv,
    gv,
    piv,
    pov,
    tls,
    qls,
    dms,
    acc,
    got_inner,
    got_outer,
    grads,
    grams,
    solved,
    load_sem,
    small_sem,
    send_outer,
    recv_outer,
    send_inner,
    recv_inner,
    send_grads,
    recv_grads,
    send_gram,
    recv_gram,
):
    me_t, me_d = lax.axis_index("tensor"), lax.axis_index("dp")
    peers_t = [lax.rem(me_t + k, tensor) for k in range(1, tensor)]
    peers_d = [lax.rem(me_d + k, dp) for k in range(1, dp)]
    rows_t, rows_q = xt.shape[0], xq.shape[0]
    rank_in, rank_out = pin.shape[0], pout.shape[0]
    share = rank_in // tensor
    width = pin.shape[1] // CHUNKS
    tokens = rows_t + rows_q

    loads = [
        pltpu.make_async_copy(gt, gv.at[pl.ds(0, rows_t), :], load_sem.at[0]),
        pltpu.make_async_copy(gq, gv.at[pl.ds(rows_t, rows_q), :], load_sem.at[1]),
        pltpu.make_async_copy(pout, pov, load_sem.at[2]),
    ]
    chunk_loads = []
    for chunk in range(CHUNKS):
        at = pl.ds(chunk * width, width)
        base = 3 + 3 * chunk
        chunk_loads.append(
            [
                pltpu.make_async_copy(xt.at[:, at], xv.at[pl.ds(0, rows_t), at], load_sem.at[base]),
                pltpu.make_async_copy(xq.at[:, at], xv.at[pl.ds(rows_t, rows_q), at], load_sem.at[base + 1]),
                pltpu.make_async_copy(pin.at[:, at], piv.at[:, at], load_sem.at[base + 2]),
            ]
        )
    small = [
        pltpu.make_async_copy(tlen, tls, small_sem.at[0]),
        pltpu.make_async_copy(qlen, qls, small_sem.at[1]),
        pltpu.make_async_copy(damp, dms, small_sem.at[2]),
    ]
    for copy in loads:
        copy.start()
    for group in chunk_loads:
        for copy in group:
            copy.start()
    for copy in small:
        copy.start()

    barrier = pltpu.get_barrier_semaphore()
    for peer in peers_t:
        pl.semaphore_signal(barrier, inc=1, device_id={"tensor": peer}, device_id_type=MESH)
    for peer in peers_d:
        pl.semaphore_signal(barrier, inc=1, device_id={"dp": peer}, device_id_type=MESH)

    acc[:, 128:] = jnp.zeros((acc.shape[0], acc.shape[1] - 128), jnp.float32)
    contract = (((1,), (1,)), ((), ()))

    for copy in loads:
        copy.wait()
    outer = lax.dot_general(pov[...], gv[...], contract, preferred_element_type=jnp.float32)
    acc[pl.ds(rank_in, rank_out), pl.ds(0, tokens)] = outer

    pl.semaphore_wait(barrier, tensor - 1 + dp - 1)
    outer_copies = []
    for k, peer in enumerate(peers_t):
        copy = pltpu.make_async_remote_copy(
            src_ref=acc.at[pl.ds(rank_in, rank_out), :],
            dst_ref=got_outer.at[k],
            send_sem=send_outer.at[k],
            recv_sem=recv_outer.at[k],
            device_id={"tensor": peer},
            device_id_type=MESH,
        )
        copy.start()
        outer_copies.append(copy)

    inner = None
    for chunk in range(CHUNKS):
        for copy in chunk_loads[chunk]:
            copy.wait()
        at = pl.ds(chunk * width, width)
        part = lax.dot_general(piv[:, at], xv[:, at], contract, preferred_element_type=jnp.float32)
        inner = part if inner is None else inner + part
    acc[pl.ds(0, rank_in), pl.ds(0, tokens)] = inner

    inner_copies = []
    for k, peer in enumerate(peers_t):
        copy = pltpu.make_async_remote_copy(
            src_ref=acc.at[pl.ds(pl.multiple_of(peer * share, share), share), :],
            dst_ref=got_inner.at[k],
            send_sem=send_inner.at[k],
            recv_sem=recv_inner.at[k],
            device_id={"tensor": peer},
            device_id_type=MESH,
        )
        copy.start()
        inner_copies.append(copy)

    for copy in small:
        copy.wait()
    row_id = lax.broadcasted_iota(jnp.int32, (ROWS, 128), 0)
    lane_id = lax.broadcasted_iota(jnp.int32, (ROWS, 128), 1)
    lengths = jnp.ones((ROWS, 128), jnp.int32)
    for e in range(8):
        lengths = jnp.where(row_id == e, tls[e], lengths)
    for e in range(query_count):
        lengths = jnp.where(row_id == 8 + e, qls[e], lengths)
    slot, example = lane_id % 16, lane_id // 16
    train_mask = (row_id < 8) & (example == row_id) & (slot < lengths)
    query_mask = (row_id >= 8) & (row_id < 8 + query_count) & (example == row_id - 8) & (slot < lengths)
    train_mask = jnp.where(train_mask, 1.0, 0.0).astype(jnp.bfloat16)
    query_mask = jnp.where(query_mask, 1.0, 0.0).astype(jnp.bfloat16)
    masks = jnp.concatenate([train_mask, query_mask, train_mask, query_mask], axis=1)
    real_lengths = lengths[:, :1].astype(jnp.float32)
    scale_code = dms[0].astype(jnp.float32) / 10.0

    outer_sum = acc[pl.ds(rank_in, rank_out), :]
    for k, copy in enumerate(outer_copies):
        copy.wait_recv()
        outer_sum = outer_sum + got_outer[k]
    inner_sum = acc[pl.ds(pl.multiple_of(me_t * share, share), share), :]
    for k, copy in enumerate(inner_copies):
        copy.wait_recv()
        inner_sum = inner_sum + got_inner[k]

    products = jnp.concatenate([inner_sum[i : i + 1, :] * outer_sum for i in range(share)], axis=0)
    high = products.astype(jnp.bfloat16)
    low = (products - high.astype(jnp.float32)).astype(jnp.bfloat16)
    summed = lax.dot_general(
        masks, jnp.concatenate([high, low], axis=1), contract, preferred_element_type=jnp.float32
    )
    mine = (summed / real_lengths).astype(jnp.bfloat16)
    grads[me_d] = mine

    grad_copies = []
    for k, peer in enumerate(peers_d):
        copy = pltpu.make_async_remote_copy(
            src_ref=grads.at[me_d],
            dst_ref=grads.at[me_d],
            send_sem=send_grads.at[k],
            recv_sem=recv_grads.at[k],
            device_id={"dp": peer},
            device_id_type=MESH,
        )
        copy.start()
        grad_copies.append(copy)
    out_train[...] = mine[:8, :]
    out_query[...] = mine[8 : 8 + query_count, :]
    for copy in grad_copies:
        copy.wait_recv()

    everyone = grads[...].reshape(dp * ROWS, mine.shape[1])
    gram = lax.dot_general(everyone, everyone, contract, preferred_element_type=jnp.float32)
    gram = jnp.concatenate([gram[d * ROWS : d * ROWS + 8, :] for d in range(dp)], axis=0)
    grams[me_t, :, pl.ds(0, dp * ROWS)] = gram
    gram_copies = []
    for k, peer in enumerate(peers_t):
        copy = pltpu.make_async_remote_copy(
            src_ref=grams.at[me_t],
            dst_ref=grams.at[me_t],
            send_sem=send_gram.at[k],
            recv_sem=recv_gram.at[k],
            device_id={"tensor": peer},
            device_id_type=MESH,
        )
        copy.start()
        gram_copies.append(copy)
    for copy in gram_copies:
        copy.wait_recv()
    whole = grams[0][:, : dp * ROWS]
    for t in range(1, tensor):
        whole = whole + grams[t][:, : dp * ROWS]

    total = dp * 8
    row = lax.broadcasted_iota(jnp.int32, whole.shape, 0)
    lane = lax.broadcasted_iota(jnp.int32, whole.shape, 1)
    diagonal = lane == (row // 8) * ROWS + row % 8
    trace = jnp.sum(jnp.where(diagonal, whole, 0.0), axis=(0, 1), keepdims=True)
    ridge = scale_code * trace / total
    system = jnp.where(diagonal, whole + ridge, whole)
    columns = [(e // 8) * ROWS + e % 8 for e in range(total)]
    solved[...] = eliminate(system, columns)
    picked = solved[pl.ds(pl.multiple_of(me_d * 8, 8), 8), :] * total
    for d in range(dp):
        out_scores[:, d * query_count : (d + 1) * query_count] = picked[
            :, d * ROWS + 8 : d * ROWS + 8 + query_count
        ]

    for copy in outer_copies + inner_copies + grad_copies + gram_copies:
        copy.wait_send()


def fused_call(x_train, gout_train, x_query, gout_query, proj_in, proj_out, train_lengths, query_lengths, damping):
    tensor, dp = lax.axis_size("tensor"), lax.axis_size("dp")
    query_count = query_lengths.shape[0]
    rank_in, rank_out = proj_in.shape[1], proj_out.shape[1]
    depth_in, depth_out = proj_in.shape[0], proj_out.shape[0]
    tokens = x_train.shape[0] + x_query.shape[0]
    share = rank_in // tensor
    features = share * rank_out
    anywhere = pl.BlockSpec(memory_space=pltpu.HBM)
    vmem = pl.BlockSpec(memory_space=pltpu.VMEM)
    dma = pltpu.SemaphoreType.DMA
    return pl.pallas_call(
        functools.partial(fused_kernel, tensor, dp, query_count),
        out_shape=(
            jax.ShapeDtypeStruct((8, features), jnp.bfloat16),
            jax.ShapeDtypeStruct((query_count, features), jnp.bfloat16),
            jax.ShapeDtypeStruct((8, dp * query_count), jnp.float32),
        ),
        in_specs=[anywhere] * 9,
        out_specs=(vmem, vmem, vmem),
        scratch_shapes=[
            pltpu.VMEM((tokens, depth_in), jnp.bfloat16),
            pltpu.VMEM((tokens, depth_out), jnp.bfloat16),
            pltpu.VMEM((rank_in, depth_in), jnp.bfloat16),
            pltpu.VMEM((rank_out, depth_out), jnp.bfloat16),
            pltpu.SMEM(train_lengths.shape, jnp.int32),
            pltpu.SMEM(query_lengths.shape, jnp.int32),
            pltpu.SMEM(damping.shape, jnp.int32),
            pltpu.VMEM((rank_in + rank_out, 256), jnp.float32),
            pltpu.VMEM((tensor - 1, share, 256), jnp.float32),
            pltpu.VMEM((tensor - 1, rank_out, 256), jnp.float32),
            pltpu.VMEM((dp, ROWS, features), jnp.bfloat16),
            pltpu.VMEM((tensor, dp * 8, 128), jnp.float32),
            pltpu.VMEM((dp * 8, dp * ROWS), jnp.float32),
            dma((3 + 3 * CHUNKS,)),
            dma((3,)),
            dma((tensor - 1,)),
            dma((tensor - 1,)),
            dma((tensor - 1,)),
            dma((tensor - 1,)),
            dma((dp - 1,)),
            dma((dp - 1,)),
            dma((tensor - 1,)),
            dma((tensor - 1,)),
        ],
        compiler_params=pltpu.CompilerParams(
            collective_id=0, has_side_effects=True, vmem_limit_bytes=60 << 20
        ),
        name="fused_scores",
    )(
        x_train,
        gout_train,
        x_query,
        gout_query,
        proj_in.T,
        proj_out.T,
        train_lengths,
        query_lengths,
        damping,
    )


def shards(
    x_train,
    gout_train,
    x_query,
    gout_query,
    proj_in,
    proj_out,
    train_lengths,
    query_lengths,
    damping,
):
    local_train = train_lengths.shape[0]
    total_train = local_train * lax.axis_size("dp")
    if fits_fused(x_train, x_query, proj_in, proj_out, train_lengths, query_lengths):
        return fused_call(
            x_train, gout_train, x_query, gout_query, proj_in, proj_out, train_lengths, query_lengths, damping
        )
    first = lax.axis_index("dp") * local_train
    scale_code = damping[0].astype(jnp.float32) / 10.0
    train_inner = jnp.dot(x_train, proj_in, preferred_element_type=jnp.float32)
    query_inner = jnp.dot(x_query, proj_in, preferred_element_type=jnp.float32)
    train_outer = jnp.dot(gout_train, proj_out, preferred_element_type=jnp.float32)
    query_outer = jnp.dot(gout_query, proj_out, preferred_element_type=jnp.float32)
    summed = lax.psum((train_inner, query_inner, train_outer, query_outer), "tensor")
    train_full = weighted_grads(summed[0], summed[2], train_lengths)
    query_full = weighted_grads(summed[1], summed[3], query_lengths)
    share = train_full.shape[1] // lax.axis_size("tensor")
    offset = lax.axis_index("tensor") * share
    train_grads = lax.dynamic_slice_in_dim(train_full, offset, share, 1)
    query_grads = lax.dynamic_slice_in_dim(query_full, offset, share, 1)
    all_train, all_query = (
        lax.all_gather(train_full, "dp", axis=0, tiled=True),
        lax.all_gather(query_full, "dp", axis=0, tiled=True),
    )
    kernel = jnp.dot(all_train, all_train.T, preferred_element_type=jnp.float32)
    cross = jnp.dot(all_train, all_query.T, preferred_element_type=jnp.float32)
    scores = kernel_scores(kernel, cross, scale_code, total_train, first, local_train)
    return (train_grads, query_grads, scores)


def solution(mesh):
    placed = (
        P(("grp", "dp"), "tensor"),
        P(("grp", "dp"), "tensor"),
        P(("grp", "dp"), "tensor"),
        P(("grp", "dp"), "tensor"),
        P("tensor", None),
        P("tensor", None),
        P(("grp", "dp")),
        P(("grp", "dp")),
        P(),
    )
    return jax.shard_map(
        shards,
        mesh=mesh,
        in_specs=placed,
        out_specs=(P(("grp", "dp"), "tensor"), P(("grp", "dp"), "tensor"), P(("grp", "dp"), None)),
        check_vma=False,
    )
```

```python
import functools

import jax
import jax.numpy as jnp
from jax import lax
from jax.experimental import pallas as pl
from jax.experimental.pallas import tpu as pltpu
from jax.sharding import PartitionSpec as P


def weighted_grads(inner, outer, lengths):
    count = lengths.shape[0]
    slots = inner.shape[0] // count
    inner = inner.reshape(count, slots, inner.shape[1])
    outer = outer.reshape(count, slots, outer.shape[1])
    valid = (lax.broadcasted_iota(jnp.int32, (count, slots), 1) < lengths[:, None]).astype(
        jnp.float32
    )
    weight = valid / lengths[:, None].astype(jnp.float32)
    summed = jnp.einsum(
        "eti,eto->eio", inner * weight[:, :, None], outer, precision=lax.Precision.HIGHEST
    )
    return summed.reshape(count, -1).astype(jnp.bfloat16)


def kernel_scores(kernel, cross, scale_code, total_train, first, local_train):
    trace = jnp.trace(kernel)
    ridge = scale_code * trace / total_train
    system = kernel + ridge * jnp.eye(total_train, dtype=jnp.float32)
    factor = jnp.linalg.cholesky(system)
    solved = jax.scipy.linalg.cho_solve((factor, True), cross)
    picked = lax.dynamic_slice_in_dim(solved, first, local_train, 0)
    return picked * total_train


MESH = pl.DeviceIdType.MESH
CHUNKS = 4
ROWS = 16


def fits_fused(x_train, x_query, proj_in, proj_out, train_lengths, query_lengths):
    train_count, query_count = train_lengths.shape[0], query_lengths.shape[0]
    tensor, dp = lax.axis_size("tensor"), lax.axis_size("dp")
    return (
        tensor > 1
        and dp > 1
        and train_count == 8
        and query_count <= 8
        and x_train.shape[0] == 128
        and x_query.shape[0] <= 128
        and 128 % x_query.shape[0] == 0
        and x_query.shape[0] // query_count == 16
        and proj_in.shape[0] % (128 * CHUNKS) == 0
        and proj_in.shape[1] % (8 * tensor) == 0
        and proj_out.shape[1] % 8 == 0
        and dp * ROWS <= 128
    )


def eliminate(system, columns):
    count = len(columns)
    row_id = lax.broadcasted_iota(jnp.int32, system.shape, 0)
    for k in range(count):
        c = columns[k]
        column = system[:, c : c + 1]
        scaled = system[k : k + 1, :] / system[k : k + 1, c : c + 1]
        system = jnp.where(row_id == k, scaled, system - column * scaled)
    return system


def packed_rows(count, lanes):
    groups = count // 8
    return -(-groups // (128 // lanes)) * 8


def pack(values):
    count, lanes = values.shape
    beside = 128 // lanes
    groups = [values[g : g + 8] for g in range(0, count, 8)]
    groups += [jnp.zeros_like(groups[0])] * (-len(groups) % beside)
    lines = [jnp.concatenate(groups[g : g + beside], axis=1) for g in range(0, len(groups), beside)]
    return jnp.concatenate(lines, axis=0) if len(lines) > 1 else lines[0]


def unpack(packed, count, lanes):
    beside = 128 // lanes
    groups = []
    for g in range(count // 8):
        line, place = packed[g // beside * 8 : g // beside * 8 + 8], g % beside
        groups.append(pltpu.roll(line, 128 - place * lanes, 1) if place else line)
    return jnp.concatenate(groups, axis=0)


def fused_kernel(
    tensor,
    dp,
    query_count,
    xt,
    gt,
    xq,
    gq,
    pin,
    pout,
    tlen,
    qlen,
    out_grads,
    out_gram,
    xv,
    gv,
    piv,
    pov,
    tls,
    qls,
    acc,
    got_inner,
    got_outer,
    grads,
    grams,
    load_sem,
    small_sem,
    send_outer,
    recv_outer,
    send_inner,
    recv_inner,
    send_grads,
    recv_grads,
    send_gram,
    recv_gram,
):
    me_t, me_d = lax.axis_index("tensor"), lax.axis_index("dp")
    peers_t = [lax.rem(me_t + k, tensor) for k in range(1, tensor)]
    peers_d = [lax.rem(me_d + k, dp) for k in range(1, dp)]
    barrier = pltpu.get_barrier_semaphore()
    for peer in peers_t:
        pl.semaphore_signal(barrier, inc=1, device_id={"tensor": peer}, device_id_type=MESH)
    for peer in peers_d:
        pl.semaphore_signal(barrier, inc=1, device_id={"dp": peer}, device_id_type=MESH)

    rows_t, rows_q = xt.shape[0], xq.shape[0]
    rank_in, rank_out = pin.shape[0], pout.shape[0]
    share = rank_in // tensor
    width = pin.shape[1] // CHUNKS
    packed_out, packed_in = packed_rows(rank_out, rows_q), packed_rows(share, rows_q)

    loads = [
        pltpu.make_async_copy(gt, gv.at[pl.ds(0, rows_t), :], load_sem.at[0]),
        pltpu.make_async_copy(gq, gv.at[pl.ds(rows_t, rows_q), :], load_sem.at[1]),
        pltpu.make_async_copy(pout, pov, load_sem.at[2]),
    ]
    chunk_loads = []
    for chunk in range(CHUNKS):
        at = pl.ds(chunk * width, width)
        base = 3 + 3 * chunk
        chunk_loads.append(
            [
                pltpu.make_async_copy(xt.at[:, at], xv.at[pl.ds(0, rows_t), at], load_sem.at[base]),
                pltpu.make_async_copy(xq.at[:, at], xv.at[pl.ds(rows_t, rows_q), at], load_sem.at[base + 1]),
                pltpu.make_async_copy(pin.at[:, at], piv.at[:, at], load_sem.at[base + 2]),
            ]
        )
    small = [
        pltpu.make_async_copy(tlen, tls, small_sem.at[0]),
        pltpu.make_async_copy(qlen, qls, small_sem.at[1]),
    ]
    for copy in loads:
        copy.start()
    for group in chunk_loads:
        for copy in group:
            copy.start()
    for copy in small:
        copy.start()

    contract = (((1,), (1,)), ((), ()))

    for copy in loads:
        copy.wait()
    outer = lax.dot_general(pov[...], gv[...], contract, preferred_element_type=jnp.float32)
    outer_rows = rank_out + packed_out
    acc[pl.ds(0, rank_out), :] = outer[:, :rows_t]
    acc[pl.ds(rank_out, packed_out), :] = pack(outer[:, rows_t:])

    inner = None
    for chunk in range(CHUNKS):
        for copy in chunk_loads[chunk]:
            copy.wait()
        at = pl.ds(chunk * width, width)
        part = lax.dot_general(piv[:, at], xv[:, at], contract, preferred_element_type=jnp.float32)
        inner = part if inner is None else inner + part
    inner_rows = share + packed_in
    for t in range(tensor):
        base = outer_rows + t * inner_rows
        acc[pl.ds(base, share), :] = inner[t * share : (t + 1) * share, :rows_t]
        acc[pl.ds(base + share, packed_in), :] = pack(inner[t * share : (t + 1) * share, rows_t:])

    pl.semaphore_wait(barrier, tensor - 1 + dp - 1)
    outer_copies, inner_copies = [], []
    for k, peer in enumerate(peers_t):
        copy = pltpu.make_async_remote_copy(
            src_ref=acc.at[pl.ds(0, outer_rows), :],
            dst_ref=got_outer.at[k],
            send_sem=send_outer.at[k],
            recv_sem=recv_outer.at[k],
            device_id={"tensor": peer},
            device_id_type=MESH,
        )
        copy.start()
        outer_copies.append(copy)
        copy = pltpu.make_async_remote_copy(
            src_ref=acc.at[pl.ds(pl.multiple_of(outer_rows + peer * inner_rows, 8), inner_rows), :],
            dst_ref=got_inner.at[k],
            send_sem=send_inner.at[k],
            recv_sem=recv_inner.at[k],
            device_id={"tensor": peer},
            device_id_type=MESH,
        )
        copy.start()
        inner_copies.append(copy)

    for copy in small:
        copy.wait()
    row_id = lax.broadcasted_iota(jnp.int32, (ROWS, 128), 0)
    lane_id = lax.broadcasted_iota(jnp.int32, (ROWS, 128), 1)
    lengths = jnp.ones((ROWS, 128), jnp.int32)
    for e in range(8):
        lengths = jnp.where(row_id == e, tls[e], lengths)
    for e in range(query_count):
        lengths = jnp.where(row_id == 8 + e, qls[e], lengths)
    slot, example = lane_id % 16, lane_id // 16
    train_mask = (row_id < 8) & (example == row_id) & (slot < lengths)
    query_mask = (row_id >= 8) & (row_id < 8 + query_count) & (example == row_id - 8) & (slot < lengths)
    train_mask = jnp.where(train_mask, 1.0, 0.0).astype(jnp.bfloat16)
    query_mask = jnp.where(query_mask, 1.0, 0.0).astype(jnp.bfloat16)
    masks = jnp.concatenate([train_mask, query_mask, train_mask, query_mask], axis=1)
    real_lengths = lengths[:, :1].astype(jnp.float32)

    outer_sum = acc[pl.ds(0, outer_rows), :]
    for k, copy in enumerate(outer_copies):
        copy.wait_recv()
        outer_sum = outer_sum + got_outer[k]
    inner_sum = acc[pl.ds(pl.multiple_of(outer_rows + me_t * inner_rows, 8), inner_rows), :]
    for k, copy in enumerate(inner_copies):
        copy.wait_recv()
        inner_sum = inner_sum + got_inner[k]

    outer_sum = jnp.concatenate([outer_sum[:rank_out], unpack(outer_sum[rank_out:], rank_out, rows_q)], axis=1)
    inner_sum = jnp.concatenate([inner_sum[:share], unpack(inner_sum[share:], share, rows_q)], axis=1)
    products = jnp.concatenate([inner_sum[i : i + 1, :] * outer_sum for i in range(share)], axis=0)
    high = products.astype(jnp.bfloat16)
    low = (products - high.astype(jnp.float32)).astype(jnp.bfloat16)
    summed = lax.dot_general(
        masks, jnp.concatenate([high, low], axis=1), contract, preferred_element_type=jnp.float32
    )
    mine = (summed / real_lengths).astype(jnp.bfloat16)
    grads[me_d] = mine

    grad_copies = []
    for k, peer in enumerate(peers_d):
        copy = pltpu.make_async_remote_copy(
            src_ref=grads.at[me_d],
            dst_ref=grads.at[me_d],
            send_sem=send_grads.at[k],
            recv_sem=recv_grads.at[k],
            device_id={"dp": peer},
            device_id_type=MESH,
        )
        copy.start()
        grad_copies.append(copy)
    out_grads[...] = mine
    for copy in grad_copies:
        copy.wait_recv()

    everyone = grads[...].reshape(dp * ROWS, mine.shape[1])
    gram = lax.dot_general(everyone, everyone, contract, preferred_element_type=jnp.float32)
    gram = jnp.concatenate([gram[d * ROWS : d * ROWS + 8, :] for d in range(dp)], axis=0)
    grams[me_t, :, pl.ds(0, dp * ROWS)] = gram
    gram_copies = []
    for k, peer in enumerate(peers_t):
        copy = pltpu.make_async_remote_copy(
            src_ref=grams.at[me_t],
            dst_ref=grams.at[me_t],
            send_sem=send_gram.at[k],
            recv_sem=recv_gram.at[k],
            device_id={"tensor": peer},
            device_id_type=MESH,
        )
        copy.start()
        gram_copies.append(copy)
    for copy in gram_copies:
        copy.wait_recv()
    whole = grams[0][:, : dp * ROWS]
    for t in range(1, tensor):
        whole = whole + grams[t][:, : dp * ROWS]

    out_gram[...] = whole
    for copy in outer_copies + inner_copies + grad_copies + gram_copies:
        copy.wait_send()


def solve_kernel(dp, query_count, mine, gram, damp, out_train, out_query, out_scores, train, query, solved, scores, dms, sems):
    me_d = lax.axis_index("dp")
    load = pltpu.make_async_copy(damp, dms, sems.at[3])
    load.start()
    train[...] = mine[pl.ds(0, 8), :]
    query[...] = mine[pl.ds(8, query_count), :]
    stores = [
        pltpu.make_async_copy(train, out_train, sems.at[0]),
        pltpu.make_async_copy(query, out_query, sems.at[1]),
        pltpu.make_async_copy(scores, out_scores, sems.at[2]),
    ]
    stores[0].start()
    stores[1].start()
    whole = gram[...]
    total = dp * 8
    row = lax.broadcasted_iota(jnp.int32, whole.shape, 0)
    lane = lax.broadcasted_iota(jnp.int32, whole.shape, 1)
    diagonal = lane == (row // 8) * ROWS + row % 8
    trace = jnp.sum(jnp.where(diagonal, whole, 0.0), axis=(0, 1), keepdims=True)
    load.wait()
    scale_code = dms[0, 0].astype(jnp.float32) / 10.0
    ridge = scale_code * trace / total
    system = jnp.where(diagonal, whole + ridge, whole)
    columns = [(e // 8) * ROWS + e % 8 for e in range(total)]
    solved[...] = eliminate(system, columns)
    picked = solved[pl.ds(pl.multiple_of(me_d * 8, 8), 8), :] * total
    for d in range(dp):
        scores[:, d * query_count : (d + 1) * query_count] = picked[
            :, d * ROWS + 8 : d * ROWS + 8 + query_count
        ]

    stores[2].start()
    for store in stores:
        store.wait()


def fused_call(x_train, gout_train, x_query, gout_query, proj_in, proj_out, train_lengths, query_lengths, damping):
    tensor, dp = lax.axis_size("tensor"), lax.axis_size("dp")
    query_count = query_lengths.shape[0]
    rank_in, rank_out = proj_in.shape[1], proj_out.shape[1]
    depth_in, depth_out = proj_in.shape[0], proj_out.shape[0]
    tokens = x_train.shape[0] + x_query.shape[0]
    share = rank_in // tensor
    features = share * rank_out
    outer_rows = rank_out + packed_rows(rank_out, x_query.shape[0])
    inner_rows = share + packed_rows(share, x_query.shape[0])
    anywhere = pl.BlockSpec(memory_space=pltpu.HBM)
    vmem = pl.BlockSpec(memory_space=pltpu.VMEM)
    dma = pltpu.SemaphoreType.DMA
    hbm = lambda array: pltpu.with_memory_space_constraint(array, pltpu.HBM)
    mine, gram = pl.pallas_call(
        functools.partial(fused_kernel, tensor, dp, query_count),
        out_shape=(
            jax.ShapeDtypeStruct((ROWS, features), jnp.bfloat16),
            jax.ShapeDtypeStruct((dp * 8, dp * ROWS), jnp.float32),
        ),
        in_specs=[anywhere] * 8,
        out_specs=(vmem, vmem),
        scratch_shapes=[
            pltpu.VMEM((tokens, depth_in), jnp.bfloat16),
            pltpu.VMEM((tokens, depth_out), jnp.bfloat16),
            pltpu.VMEM((rank_in, depth_in), jnp.bfloat16),
            pltpu.VMEM((rank_out, depth_out), jnp.bfloat16),
            pltpu.SMEM(train_lengths.shape, jnp.int32),
            pltpu.SMEM(query_lengths.shape, jnp.int32),
            pltpu.VMEM((outer_rows + tensor * inner_rows, 128), jnp.float32),
            pltpu.VMEM((tensor - 1, inner_rows, 128), jnp.float32),
            pltpu.VMEM((tensor - 1, outer_rows, 128), jnp.float32),
            pltpu.VMEM((dp, ROWS, features), jnp.bfloat16),
            pltpu.VMEM((tensor, dp * 8, 128), jnp.float32),
            dma((3 + 3 * CHUNKS,)),
            dma((2,)),
            dma((tensor - 1,)),
            dma((tensor - 1,)),
            dma((tensor - 1,)),
            dma((tensor - 1,)),
            dma((dp - 1,)),
            dma((dp - 1,)),
            dma((tensor - 1,)),
            dma((tensor - 1,)),
        ],
        compiler_params=pltpu.CompilerParams(
            collective_id=0, has_side_effects=True, vmem_limit_bytes=16 << 20
        ),
        name="fused_grams",
    )(
        hbm(x_train),
        hbm(gout_train),
        hbm(x_query),
        hbm(gout_query),
        hbm(proj_in.T),
        hbm(proj_out.T),
        hbm(train_lengths),
        hbm(query_lengths),
    )
    return pl.pallas_call(
        functools.partial(solve_kernel, dp, query_count),
        out_shape=(
            jax.ShapeDtypeStruct((8, features), jnp.bfloat16),
            jax.ShapeDtypeStruct((query_count, features), jnp.bfloat16),
            jax.ShapeDtypeStruct((8, dp * query_count), jnp.float32),
        ),
        in_specs=[vmem, vmem, anywhere],
        out_specs=[anywhere] * 3,
        scratch_shapes=[
            pltpu.VMEM((8, features), jnp.bfloat16),
            pltpu.VMEM((query_count, features), jnp.bfloat16),
            pltpu.VMEM((dp * 8, dp * ROWS), jnp.float32),
            pltpu.VMEM((8, dp * query_count), jnp.float32),
            pltpu.SMEM((1, 1), jnp.int32),
            dma((4,)),
        ],
        name="solve_scores",
    )(
        pltpu.with_memory_space_constraint(mine, pltpu.VMEM),
        pltpu.with_memory_space_constraint(gram, pltpu.VMEM),
        damping.reshape(1, 1),
    )


def shards(
    x_train,
    gout_train,
    x_query,
    gout_query,
    proj_in,
    proj_out,
    train_lengths,
    query_lengths,
    damping,
):
    local_train = train_lengths.shape[0]
    total_train = local_train * lax.axis_size("dp")
    if fits_fused(x_train, x_query, proj_in, proj_out, train_lengths, query_lengths):
        return fused_call(
            x_train, gout_train, x_query, gout_query, proj_in, proj_out, train_lengths, query_lengths, damping
        )
    first = lax.axis_index("dp") * local_train
    scale_code = damping[0].astype(jnp.float32) / 10.0
    train_inner = jnp.dot(x_train, proj_in, preferred_element_type=jnp.float32)
    query_inner = jnp.dot(x_query, proj_in, preferred_element_type=jnp.float32)
    train_outer = jnp.dot(gout_train, proj_out, preferred_element_type=jnp.float32)
    query_outer = jnp.dot(gout_query, proj_out, preferred_element_type=jnp.float32)
    summed = lax.psum((train_inner, query_inner, train_outer, query_outer), "tensor")
    train_full = weighted_grads(summed[0], summed[2], train_lengths)
    query_full = weighted_grads(summed[1], summed[3], query_lengths)
    share = train_full.shape[1] // lax.axis_size("tensor")
    offset = lax.axis_index("tensor") * share
    train_grads = lax.dynamic_slice_in_dim(train_full, offset, share, 1)
    query_grads = lax.dynamic_slice_in_dim(query_full, offset, share, 1)
    all_train, all_query = (
        lax.all_gather(train_full, "dp", axis=0, tiled=True),
        lax.all_gather(query_full, "dp", axis=0, tiled=True),
    )
    kernel = jnp.dot(all_train, all_train.T, preferred_element_type=jnp.float32)
    cross = jnp.dot(all_train, all_query.T, preferred_element_type=jnp.float32)
    scores = kernel_scores(kernel, cross, scale_code, total_train, first, local_train)
    return (train_grads, query_grads, scores)


def solution(mesh):
    placed = (
        P(("grp", "dp"), "tensor"),
        P(("grp", "dp"), "tensor"),
        P(("grp", "dp"), "tensor"),
        P(("grp", "dp"), "tensor"),
        P("tensor", None),
        P("tensor", None),
        P(("grp", "dp")),
        P(("grp", "dp")),
        P(),
    )
    return jax.shard_map(
        shards,
        mesh=mesh,
        in_specs=placed,
        out_specs=(P(("grp", "dp"), "tensor"), P(("grp", "dp"), "tensor"), P(("grp", "dp"), None)),
        check_vma=False,
    )
```

```python
import functools

import jax
import jax.numpy as jnp
from jax import lax
from jax.experimental import pallas as pl
from jax.experimental.pallas import tpu as pltpu
from jax.sharding import PartitionSpec as P


def weighted_grads(inner, outer, lengths):
    count = lengths.shape[0]
    slots = inner.shape[0] // count
    inner = inner.reshape(count, slots, inner.shape[1])
    outer = outer.reshape(count, slots, outer.shape[1])
    valid = (lax.broadcasted_iota(jnp.int32, (count, slots), 1) < lengths[:, None]).astype(
        jnp.float32
    )
    weight = valid / lengths[:, None].astype(jnp.float32)
    summed = jnp.einsum(
        "eti,eto->eio", inner * weight[:, :, None], outer, precision=lax.Precision.HIGHEST
    )
    return summed.reshape(count, -1).astype(jnp.bfloat16)


def kernel_scores(kernel, cross, scale_code, total_train, first, local_train):
    trace = jnp.trace(kernel)
    ridge = scale_code * trace / total_train
    system = kernel + ridge * jnp.eye(total_train, dtype=jnp.float32)
    factor = jnp.linalg.cholesky(system)
    solved = jax.scipy.linalg.cho_solve((factor, True), cross)
    picked = lax.dynamic_slice_in_dim(solved, first, local_train, 0)
    return picked * total_train


MESH = pl.DeviceIdType.MESH
CHUNKS = 4
ROWS = 16


def fits_fused(x_train, x_query, proj_in, proj_out, train_lengths, query_lengths):
    train_count, query_count = train_lengths.shape[0], query_lengths.shape[0]
    tensor, dp = lax.axis_size("tensor"), lax.axis_size("dp")
    return (
        tensor > 1
        and dp > 1
        and train_count == 8
        and query_count <= 8
        and x_train.shape[0] == 128
        and x_query.shape[0] <= 128
        and 128 % x_query.shape[0] == 0
        and x_query.shape[0] // query_count == 16
        and proj_in.shape[0] % (128 * CHUNKS) == 0
        and proj_in.shape[1] % (8 * tensor) == 0
        and proj_out.shape[1] % 8 == 0
        and dp * ROWS <= 128
    )


def eliminate(system, columns):
    shape = system.shape
    row_id = lax.broadcasted_iota(jnp.int32, shape, 0)

    def inverse_of(first, second, k):
        a, b = first[k : k + 1], second[k : k + 1]
        c, d = first[k + 1 : k + 2], second[k + 1 : k + 2]
        factor = 1.0 / (a * d - b * c)
        a, b, c, d = a * factor, b * factor, c * factor, d * factor
        return lambda top, bottom: (d * top - b * bottom, a * bottom - c * top)

    def cleared(values, first, second, top, bottom, k):
        rest = values - first * top - second * bottom
        return jnp.where(row_id == k, top, jnp.where(row_id == k + 1, bottom, rest))

    for k in range(0, len(columns), 4):
        c0, c1, c2, c3 = [jnp.broadcast_to(system[:, c : c + 1], shape) for c in columns[k : k + 4]]
        apply = inverse_of(c0, c1, k)
        top, bottom = apply(system[k : k + 1], system[k + 1 : k + 2])
        c2 = cleared(c2, c0, c1, *apply(c2[k : k + 1], c2[k + 1 : k + 2]), k)
        c3 = cleared(c3, c0, c1, *apply(c3[k : k + 1], c3[k + 1 : k + 2]), k)
        system = cleared(system, c0, c1, top, bottom, k)
        apply = inverse_of(c2, c3, k + 2)
        top, bottom = apply(system[k + 2 : k + 3], system[k + 3 : k + 4])
        system = cleared(system, c2, c3, top, bottom, k + 2)
    return system


def packed_rows(count, lanes):
    groups = count // 8
    return -(-groups // (128 // lanes)) * 8


def pack(values):
    count, lanes = values.shape
    beside = 128 // lanes
    groups = [values[g : g + 8] for g in range(0, count, 8)]
    groups += [jnp.zeros_like(groups[0])] * (-len(groups) % beside)
    lines = [jnp.concatenate(groups[g : g + beside], axis=1) for g in range(0, len(groups), beside)]
    return jnp.concatenate(lines, axis=0) if len(lines) > 1 else lines[0]


def unpack(packed, count, lanes):
    beside = 128 // lanes
    groups = []
    for g in range(count // 8):
        line, place = packed[g // beside * 8 : g // beside * 8 + 8], g % beside
        groups.append(pltpu.roll(line, 128 - place * lanes, 1) if place else line)
    return jnp.concatenate(groups, axis=0)


def fused_kernel(
    tensor,
    dp,
    query_count,
    xt,
    gt,
    xq,
    gq,
    pin,
    pout,
    tlen,
    qlen,
    out_grads,
    out_gram,
    xv,
    gv,
    piv,
    pov,
    tls,
    qls,
    acc,
    got_inner,
    got_outer,
    grads,
    grams,
    load_sem,
    small_sem,
    send_outer,
    recv_outer,
    send_inner,
    recv_inner,
    send_grads,
    recv_grads,
    send_gram,
    recv_gram,
):
    me_t, me_d = lax.axis_index("tensor"), lax.axis_index("dp")
    peers_t = [lax.rem(me_t + k, tensor) for k in range(1, tensor)]
    peers_d = [lax.rem(me_d + k, dp) for k in range(1, dp)]
    barrier = pltpu.get_barrier_semaphore()
    for peer in peers_t:
        pl.semaphore_signal(barrier, inc=1, device_id={"tensor": peer}, device_id_type=MESH)
    for peer in peers_d:
        pl.semaphore_signal(barrier, inc=1, device_id={"dp": peer}, device_id_type=MESH)

    rows_t, rows_q = xt.shape[0], xq.shape[0]
    rank_in, rank_out = pin.shape[0], pout.shape[0]
    share = rank_in // tensor
    width = pin.shape[1] // CHUNKS
    packed_out, packed_in = packed_rows(rank_out, rows_q), packed_rows(share, rows_q)

    loads = [
        pltpu.make_async_copy(gt, gv.at[pl.ds(0, rows_t), :], load_sem.at[0]),
        pltpu.make_async_copy(gq, gv.at[pl.ds(rows_t, rows_q), :], load_sem.at[1]),
        pltpu.make_async_copy(pout, pov, load_sem.at[2]),
    ]
    chunk_loads = []
    for chunk in range(CHUNKS):
        at = pl.ds(chunk * width, width)
        base = 3 + 3 * chunk
        chunk_loads.append(
            [
                pltpu.make_async_copy(xt.at[:, at], xv.at[pl.ds(0, rows_t), at], load_sem.at[base]),
                pltpu.make_async_copy(xq.at[:, at], xv.at[pl.ds(rows_t, rows_q), at], load_sem.at[base + 1]),
                pltpu.make_async_copy(pin.at[:, at], piv.at[:, at], load_sem.at[base + 2]),
            ]
        )
    small = [
        pltpu.make_async_copy(tlen, tls, small_sem.at[0]),
        pltpu.make_async_copy(qlen, qls, small_sem.at[1]),
    ]
    for copy in loads:
        copy.start()
    for group in chunk_loads:
        for copy in group:
            copy.start()
    for copy in small:
        copy.start()

    contract = (((1,), (1,)), ((), ()))

    for copy in loads:
        copy.wait()
    outer = lax.dot_general(pov[...], gv[...], contract, preferred_element_type=jnp.float32)
    outer_rows = rank_out + packed_out
    acc[pl.ds(0, rank_out), :] = outer[:, :rows_t]
    acc[pl.ds(rank_out, packed_out), :] = pack(outer[:, rows_t:])

    inner = None
    for chunk in range(CHUNKS):
        for copy in chunk_loads[chunk]:
            copy.wait()
        at = pl.ds(chunk * width, width)
        part = lax.dot_general(piv[:, at], xv[:, at], contract, preferred_element_type=jnp.float32)
        inner = part if inner is None else inner + part
    inner_rows = share + packed_in
    for t in range(tensor):
        base = outer_rows + t * inner_rows
        acc[pl.ds(base, share), :] = inner[t * share : (t + 1) * share, :rows_t]
        acc[pl.ds(base + share, packed_in), :] = pack(inner[t * share : (t + 1) * share, rows_t:])

    pl.semaphore_wait(barrier, tensor - 1 + dp - 1)
    outer_copies, inner_copies = [], []
    for k, peer in enumerate(peers_t):
        copy = pltpu.make_async_remote_copy(
            src_ref=acc.at[pl.ds(0, outer_rows), :],
            dst_ref=got_outer.at[k],
            send_sem=send_outer.at[k],
            recv_sem=recv_outer.at[k],
            device_id={"tensor": peer},
            device_id_type=MESH,
        )
        copy.start()
        outer_copies.append(copy)
        copy = pltpu.make_async_remote_copy(
            src_ref=acc.at[pl.ds(pl.multiple_of(outer_rows + peer * inner_rows, 8), inner_rows), :],
            dst_ref=got_inner.at[k],
            send_sem=send_inner.at[k],
            recv_sem=recv_inner.at[k],
            device_id={"tensor": peer},
            device_id_type=MESH,
        )
        copy.start()
        inner_copies.append(copy)

    for copy in small:
        copy.wait()
    row_id = lax.broadcasted_iota(jnp.int32, (ROWS, 128), 0)
    lane_id = lax.broadcasted_iota(jnp.int32, (ROWS, 128), 1)
    lengths = jnp.ones((ROWS, 128), jnp.int32)
    for e in range(8):
        lengths = jnp.where(row_id == e, tls[e], lengths)
    for e in range(query_count):
        lengths = jnp.where(row_id == 8 + e, qls[e], lengths)
    slot, example = lane_id % 16, lane_id // 16
    train_mask = (row_id < 8) & (example == row_id) & (slot < lengths)
    query_mask = (row_id >= 8) & (row_id < 8 + query_count) & (example == row_id - 8) & (slot < lengths)
    train_mask = jnp.where(train_mask, 1.0, 0.0).astype(jnp.bfloat16)
    query_mask = jnp.where(query_mask, 1.0, 0.0).astype(jnp.bfloat16)
    masks = jnp.concatenate([train_mask, query_mask, train_mask, query_mask], axis=1)
    real_lengths = lengths[:, :1].astype(jnp.float32)

    outer_sum = acc[pl.ds(0, outer_rows), :]
    for k, copy in enumerate(outer_copies):
        copy.wait_recv()
        outer_sum = outer_sum + got_outer[k]
    inner_sum = acc[pl.ds(pl.multiple_of(outer_rows + me_t * inner_rows, 8), inner_rows), :]
    for k, copy in enumerate(inner_copies):
        copy.wait_recv()
        inner_sum = inner_sum + got_inner[k]

    outer_sum = jnp.concatenate([outer_sum[:rank_out], unpack(outer_sum[rank_out:], rank_out, rows_q)], axis=1)
    inner_sum = jnp.concatenate([inner_sum[:share], unpack(inner_sum[share:], share, rows_q)], axis=1)
    products = jnp.concatenate([inner_sum[i : i + 1, :] * outer_sum for i in range(share)], axis=0)
    high = products.astype(jnp.bfloat16)
    low = (products - high.astype(jnp.float32)).astype(jnp.bfloat16)
    summed = lax.dot_general(
        masks, jnp.concatenate([high, low], axis=1), contract, preferred_element_type=jnp.float32
    )
    mine = (summed / real_lengths).astype(jnp.bfloat16)
    grads[me_d] = mine

    grad_copies = []
    for k, peer in enumerate(peers_d):
        copy = pltpu.make_async_remote_copy(
            src_ref=grads.at[me_d],
            dst_ref=grads.at[me_d],
            send_sem=send_grads.at[k],
            recv_sem=recv_grads.at[k],
            device_id={"dp": peer},
            device_id_type=MESH,
        )
        copy.start()
        grad_copies.append(copy)
    out_grads[...] = mine
    for copy in grad_copies:
        copy.wait_recv()

    everyone = grads[...].reshape(dp * ROWS, mine.shape[1])
    gram = lax.dot_general(everyone, everyone, contract, preferred_element_type=jnp.float32)
    gram = jnp.concatenate([gram[d * ROWS : d * ROWS + 8, :] for d in range(dp)], axis=0)
    grams[me_t, :, pl.ds(0, dp * ROWS)] = gram
    gram_copies = []
    for k, peer in enumerate(peers_t):
        copy = pltpu.make_async_remote_copy(
            src_ref=grams.at[me_t],
            dst_ref=grams.at[me_t],
            send_sem=send_gram.at[k],
            recv_sem=recv_gram.at[k],
            device_id={"tensor": peer},
            device_id_type=MESH,
        )
        copy.start()
        gram_copies.append(copy)
    for copy in gram_copies:
        copy.wait_recv()
    whole = grams[0][:, : dp * ROWS]
    for t in range(1, tensor):
        whole = whole + grams[t][:, : dp * ROWS]

    out_gram[...] = whole
    for copy in outer_copies + inner_copies + grad_copies + gram_copies:
        copy.wait_send()


def solve_kernel(dp, query_count, mine, gram, damp, out_train, out_query, out_scores, train, query, solved, scores, sems):
    me_d = lax.axis_index("dp")
    train[...] = mine[pl.ds(0, 8), :]
    query[...] = mine[pl.ds(8, query_count), :]
    stores = [
        pltpu.make_async_copy(train, out_train, sems.at[0]),
        pltpu.make_async_copy(query, out_query, sems.at[1]),
        pltpu.make_async_copy(scores, out_scores, sems.at[2]),
    ]
    stores[0].start()
    stores[1].start()
    whole = gram[...]
    total = dp * 8
    row = lax.broadcasted_iota(jnp.int32, whole.shape, 0)
    lane = lax.broadcasted_iota(jnp.int32, whole.shape, 1)
    diagonal = lane == (row // 8) * ROWS + row % 8
    trace = jnp.sum(jnp.where(diagonal, whole, 0.0), axis=(0, 1), keepdims=True)
    scale_code = damp[0:1, 0:1].astype(jnp.float32) / 10.0
    system = whole / trace
    system = jnp.where(diagonal, system + scale_code / total, system)
    columns = [(e // 8) * ROWS + e % 8 for e in range(total)]
    solved[...] = eliminate(system, columns)
    picked = solved[pl.ds(pl.multiple_of(me_d * 8, 8), 8), :] * total
    for d in range(dp):
        scores[:, d * query_count : (d + 1) * query_count] = picked[
            :, d * ROWS + 8 : d * ROWS + 8 + query_count
        ]

    stores[2].start()
    for store in stores:
        store.wait()


def fused_call(x_train, gout_train, x_query, gout_query, proj_in, proj_out, train_lengths, query_lengths, damping):
    tensor, dp = lax.axis_size("tensor"), lax.axis_size("dp")
    query_count = query_lengths.shape[0]
    rank_in, rank_out = proj_in.shape[1], proj_out.shape[1]
    depth_in, depth_out = proj_in.shape[0], proj_out.shape[0]
    tokens = x_train.shape[0] + x_query.shape[0]
    share = rank_in // tensor
    features = share * rank_out
    outer_rows = rank_out + packed_rows(rank_out, x_query.shape[0])
    inner_rows = share + packed_rows(share, x_query.shape[0])
    anywhere = pl.BlockSpec(memory_space=pltpu.HBM)
    vmem = pl.BlockSpec(memory_space=pltpu.VMEM)
    dma = pltpu.SemaphoreType.DMA
    hbm = lambda array: pltpu.with_memory_space_constraint(array, pltpu.HBM)
    mine, gram = pl.pallas_call(
        functools.partial(fused_kernel, tensor, dp, query_count),
        out_shape=(
            jax.ShapeDtypeStruct((ROWS, features), jnp.bfloat16),
            jax.ShapeDtypeStruct((dp * 8, dp * ROWS), jnp.float32),
        ),
        in_specs=[anywhere] * 8,
        out_specs=(vmem, vmem),
        scratch_shapes=[
            pltpu.VMEM((tokens, depth_in), jnp.bfloat16),
            pltpu.VMEM((tokens, depth_out), jnp.bfloat16),
            pltpu.VMEM((rank_in, depth_in), jnp.bfloat16),
            pltpu.VMEM((rank_out, depth_out), jnp.bfloat16),
            pltpu.SMEM(train_lengths.shape, jnp.int32),
            pltpu.SMEM(query_lengths.shape, jnp.int32),
            pltpu.VMEM((outer_rows + tensor * inner_rows, 128), jnp.float32),
            pltpu.VMEM((tensor - 1, inner_rows, 128), jnp.float32),
            pltpu.VMEM((tensor - 1, outer_rows, 128), jnp.float32),
            pltpu.VMEM((dp, ROWS, features), jnp.bfloat16),
            pltpu.VMEM((tensor, dp * 8, 128), jnp.float32),
            dma((3 + 3 * CHUNKS,)),
            dma((2,)),
            dma((tensor - 1,)),
            dma((tensor - 1,)),
            dma((tensor - 1,)),
            dma((tensor - 1,)),
            dma((dp - 1,)),
            dma((dp - 1,)),
            dma((tensor - 1,)),
            dma((tensor - 1,)),
        ],
        compiler_params=pltpu.CompilerParams(
            collective_id=0, has_side_effects=True, vmem_limit_bytes=16 << 20
        ),
        name="fused_grams",
    )(
        hbm(x_train),
        hbm(gout_train),
        hbm(x_query),
        hbm(gout_query),
        hbm(proj_in.T),
        hbm(proj_out.T),
        hbm(train_lengths),
        hbm(query_lengths),
    )
    return pl.pallas_call(
        functools.partial(solve_kernel, dp, query_count),
        out_shape=(
            jax.ShapeDtypeStruct((8, features), jnp.bfloat16),
            jax.ShapeDtypeStruct((query_count, features), jnp.bfloat16),
            jax.ShapeDtypeStruct((8, dp * query_count), jnp.float32),
        ),
        in_specs=[vmem, vmem, vmem],
        out_specs=[anywhere] * 3,
        scratch_shapes=[
            pltpu.VMEM((8, features), jnp.bfloat16),
            pltpu.VMEM((query_count, features), jnp.bfloat16),
            pltpu.VMEM((dp * 8, dp * ROWS), jnp.float32),
            pltpu.VMEM((8, dp * query_count), jnp.float32),
            dma((3,)),
        ],
        name="solve_scores",
    )(
        pltpu.with_memory_space_constraint(mine, pltpu.VMEM),
        pltpu.with_memory_space_constraint(gram, pltpu.VMEM),
        pltpu.with_memory_space_constraint(jnp.broadcast_to(damping, (8, 128)), pltpu.VMEM),
    )


def shards(
    x_train,
    gout_train,
    x_query,
    gout_query,
    proj_in,
    proj_out,
    train_lengths,
    query_lengths,
    damping,
):
    local_train = train_lengths.shape[0]
    total_train = local_train * lax.axis_size("dp")
    if fits_fused(x_train, x_query, proj_in, proj_out, train_lengths, query_lengths):
        return fused_call(
            x_train, gout_train, x_query, gout_query, proj_in, proj_out, train_lengths, query_lengths, damping
        )
    first = lax.axis_index("dp") * local_train
    scale_code = damping[0].astype(jnp.float32) / 10.0
    train_inner = jnp.dot(x_train, proj_in, preferred_element_type=jnp.float32)
    query_inner = jnp.dot(x_query, proj_in, preferred_element_type=jnp.float32)
    train_outer = jnp.dot(gout_train, proj_out, preferred_element_type=jnp.float32)
    query_outer = jnp.dot(gout_query, proj_out, preferred_element_type=jnp.float32)
    summed = lax.psum((train_inner, query_inner, train_outer, query_outer), "tensor")
    train_full = weighted_grads(summed[0], summed[2], train_lengths)
    query_full = weighted_grads(summed[1], summed[3], query_lengths)
    share = train_full.shape[1] // lax.axis_size("tensor")
    offset = lax.axis_index("tensor") * share
    train_grads = lax.dynamic_slice_in_dim(train_full, offset, share, 1)
    query_grads = lax.dynamic_slice_in_dim(query_full, offset, share, 1)
    all_train, all_query = (
        lax.all_gather(train_full, "dp", axis=0, tiled=True),
        lax.all_gather(query_full, "dp", axis=0, tiled=True),
    )
    kernel = jnp.dot(all_train, all_train.T, preferred_element_type=jnp.float32)
    cross = jnp.dot(all_train, all_query.T, preferred_element_type=jnp.float32)
    scores = kernel_scores(kernel, cross, scale_code, total_train, first, local_train)
    return (train_grads, query_grads, scores)


def solution(mesh):
    placed = (
        P(("grp", "dp"), "tensor"),
        P(("grp", "dp"), "tensor"),
        P(("grp", "dp"), "tensor"),
        P(("grp", "dp"), "tensor"),
        P("tensor", None),
        P("tensor", None),
        P(("grp", "dp")),
        P(("grp", "dp")),
        P(),
    )
    return jax.shard_map(
        shards,
        mesh=mesh,
        in_specs=placed,
        out_specs=(P(("grp", "dp"), "tensor"), P(("grp", "dp"), "tensor"), P(("grp", "dp"), None)),
        check_vma=False,
    )
```

```python
import functools

import jax
import jax.numpy as jnp
from jax import lax
from jax.experimental import pallas as pl
from jax.experimental.pallas import tpu as pltpu
from jax.sharding import PartitionSpec as P


def weighted_grads(inner, outer, lengths):
    count = lengths.shape[0]
    slots = inner.shape[0] // count
    inner = inner.reshape(count, slots, inner.shape[1])
    outer = outer.reshape(count, slots, outer.shape[1])
    valid = (lax.broadcasted_iota(jnp.int32, (count, slots), 1) < lengths[:, None]).astype(
        jnp.float32
    )
    weight = valid / lengths[:, None].astype(jnp.float32)
    summed = jnp.einsum(
        "eti,eto->eio", inner * weight[:, :, None], outer, precision=lax.Precision.HIGHEST
    )
    return summed.reshape(count, -1).astype(jnp.bfloat16)


def kernel_scores(kernel, cross, scale_code, total_train, first, local_train):
    trace = jnp.trace(kernel)
    ridge = scale_code * trace / total_train
    system = kernel + ridge * jnp.eye(total_train, dtype=jnp.float32)
    factor = jnp.linalg.cholesky(system)
    solved = jax.scipy.linalg.cho_solve((factor, True), cross)
    picked = lax.dynamic_slice_in_dim(solved, first, local_train, 0)
    return picked * total_train


MESH = pl.DeviceIdType.MESH
CHUNKS = 4
ROWS = 16


def fits_fused(x_train, x_query, proj_in, proj_out, train_lengths, query_lengths):
    train_count, query_count = train_lengths.shape[0], query_lengths.shape[0]
    tensor, dp = lax.axis_size("tensor"), lax.axis_size("dp")
    return (
        tensor > 1
        and tensor % 2 == 0
        and dp > 1
        and train_count == 8
        and query_count <= 8
        and x_train.shape[0] == 128
        and x_query.shape[0] <= 128
        and 128 % x_query.shape[0] == 0
        and x_query.shape[0] // query_count == 16
        and proj_in.shape[0] % (128 * CHUNKS) == 0
        and proj_in.shape[1] % (8 * tensor) == 0
        and proj_out.shape[1] % 8 == 0
        and dp * ROWS <= 128
    )


def eliminate(system, columns):
    shape = system.shape
    row_id = lax.broadcasted_iota(jnp.int32, shape, 0)

    def inverse_of(first, second, k):
        a, b = first[k : k + 1], second[k : k + 1]
        c, d = first[k + 1 : k + 2], second[k + 1 : k + 2]
        factor = 1.0 / (a * d - b * c)
        a, b, c, d = a * factor, b * factor, c * factor, d * factor
        return lambda top, bottom: (d * top - b * bottom, a * bottom - c * top)

    def cleared(values, first, second, top, bottom, k):
        rest = values - first * top - second * bottom
        return jnp.where(row_id == k, top, jnp.where(row_id == k + 1, bottom, rest))

    for k in range(0, len(columns), 4):
        c0, c1, c2, c3 = [jnp.broadcast_to(system[:, c : c + 1], shape) for c in columns[k : k + 4]]
        apply = inverse_of(c0, c1, k)
        top, bottom = apply(system[k : k + 1], system[k + 1 : k + 2])
        c2 = cleared(c2, c0, c1, *apply(c2[k : k + 1], c2[k + 1 : k + 2]), k)
        c3 = cleared(c3, c0, c1, *apply(c3[k : k + 1], c3[k + 1 : k + 2]), k)
        system = cleared(system, c0, c1, top, bottom, k)
        apply = inverse_of(c2, c3, k + 2)
        top, bottom = apply(system[k + 2 : k + 3], system[k + 3 : k + 4])
        system = cleared(system, c2, c3, top, bottom, k + 2)
    return system


def packed_rows(count, lanes):
    groups = count // 8
    return -(-groups // (128 // lanes)) * 8


def pack(values):
    count, lanes = values.shape
    beside = 128 // lanes
    groups = [values[g : g + 8] for g in range(0, count, 8)]
    groups += [jnp.zeros_like(groups[0])] * (-len(groups) % beside)
    lines = [jnp.concatenate(groups[g : g + beside], axis=1) for g in range(0, len(groups), beside)]
    return jnp.concatenate(lines, axis=0) if len(lines) > 1 else lines[0]


def unpack(packed, count, lanes):
    beside = 128 // lanes
    groups = []
    for g in range(count // 8):
        line, place = packed[g // beside * 8 : g // beside * 8 + 8], g % beside
        groups.append(pltpu.roll(line, 128 - place * lanes, 1) if place else line)
    return jnp.concatenate(groups, axis=0)


def fused_kernel(
    tensor,
    dp,
    query_count,
    xt,
    gt,
    xq,
    gq,
    pin,
    pout,
    tlen,
    qlen,
    out_grads,
    out_gram,
    xv,
    gv,
    piv,
    pov,
    tls,
    qls,
    acc,
    got_inner,
    got_outer,
    grads,
    grams,
    load_sem,
    small_sem,
    send_outer,
    recv_outer,
    send_inner,
    recv_inner,
    send_grads,
    recv_grads,
    send_gram,
    recv_gram,
):
    me_t, me_d = lax.axis_index("tensor"), lax.axis_index("dp")
    peers_t = [lax.rem(me_t + k, tensor) for k in range(1, tensor)]
    peers_d = [lax.rem(me_d + k, dp) for k in range(1, dp)]
    barrier = pltpu.get_barrier_semaphore()
    for peer in peers_t:
        pl.semaphore_signal(barrier, inc=1, device_id={"tensor": peer}, device_id_type=MESH)
    for peer in peers_d:
        pl.semaphore_signal(barrier, inc=1, device_id={"dp": peer}, device_id_type=MESH)

    rows_t, rows_q = xt.shape[0], xq.shape[0]
    rank_in, rank_out = pin.shape[0], pout.shape[0]
    share = rank_in // tensor
    width = pin.shape[1] // CHUNKS
    packed_out, packed_in = packed_rows(rank_out, rows_q), packed_rows(share, rows_q)

    loads = [
        pltpu.make_async_copy(gt, gv.at[pl.ds(0, rows_t), :], load_sem.at[0]),
        pltpu.make_async_copy(gq, gv.at[pl.ds(rows_t, rows_q), :], load_sem.at[1]),
        pltpu.make_async_copy(pout, pov, load_sem.at[2]),
    ]
    chunk_loads = []
    for chunk in range(CHUNKS):
        at = pl.ds(chunk * width, width)
        base = 3 + 3 * chunk
        chunk_loads.append(
            [
                pltpu.make_async_copy(xt.at[:, at], xv.at[pl.ds(0, rows_t), at], load_sem.at[base]),
                pltpu.make_async_copy(xq.at[:, at], xv.at[pl.ds(rows_t, rows_q), at], load_sem.at[base + 1]),
                pltpu.make_async_copy(pin.at[:, at], piv.at[:, at], load_sem.at[base + 2]),
            ]
        )
    small = [
        pltpu.make_async_copy(tlen, tls, small_sem.at[0]),
        pltpu.make_async_copy(qlen, qls, small_sem.at[1]),
    ]
    for copy in loads:
        copy.start()
    for group in chunk_loads:
        for copy in group:
            copy.start()
    for copy in small:
        copy.start()

    contract = (((1,), (1,)), ((), ()))

    for copy in loads:
        copy.wait()
    outer = lax.dot_general(pov[...], gv[...], contract, preferred_element_type=jnp.float32)
    outer_rows = rank_out + packed_out
    acc[pl.ds(0, rank_out), :] = outer[:, :rows_t]
    acc[pl.ds(rank_out, packed_out), :] = pack(outer[:, rows_t:])

    inner = None
    for chunk in range(CHUNKS):
        for copy in chunk_loads[chunk]:
            copy.wait()
        at = pl.ds(chunk * width, width)
        part = lax.dot_general(piv[:, at], xv[:, at], contract, preferred_element_type=jnp.float32)
        inner = part if inner is None else inner + part
    inner_rows = share + packed_in
    half = tensor // 2
    both_rows = half * inner_rows
    for t in range(tensor):
        base = outer_rows + (t % 2 * half + t // 2) * inner_rows
        acc[pl.ds(base, share), :] = inner[t * share : (t + 1) * share, :rows_t]
        acc[pl.ds(base + share, packed_in), :] = pack(inner[t * share : (t + 1) * share, rows_t:])

    pl.semaphore_wait(barrier, tensor - 1 + dp - 1)
    outer_copies, inner_copies = [], []
    for k, peer in enumerate(peers_t):
        copy = pltpu.make_async_remote_copy(
            src_ref=acc.at[pl.ds(0, outer_rows), :],
            dst_ref=got_outer.at[me_t],
            send_sem=send_outer.at[k],
            recv_sem=recv_outer.at[k],
            device_id={"tensor": peer},
            device_id_type=MESH,
        )
        copy.start()
        outer_copies.append(copy)
        copy = pltpu.make_async_remote_copy(
            src_ref=acc.at[pl.ds(pl.multiple_of(outer_rows + lax.rem(peer, 2) * both_rows, 8), both_rows), :],
            dst_ref=got_inner.at[me_t],
            send_sem=send_inner.at[k],
            recv_sem=recv_inner.at[k],
            device_id={"tensor": peer},
            device_id_type=MESH,
        )
        copy.start()
        inner_copies.append(copy)

    for copy in small:
        copy.wait()
    row_id = lax.broadcasted_iota(jnp.int32, (ROWS, 128), 0)
    lane_id = lax.broadcasted_iota(jnp.int32, (ROWS, 128), 1)
    lengths = jnp.ones((ROWS, 128), jnp.int32)
    for e in range(8):
        lengths = jnp.where(row_id == e, tls[e], lengths)
    for e in range(query_count):
        lengths = jnp.where(row_id == 8 + e, qls[e], lengths)
    slot, example = lane_id % 16, lane_id // 16
    train_mask = (row_id < 8) & (example == row_id) & (slot < lengths)
    query_mask = (row_id >= 8) & (row_id < 8 + query_count) & (example == row_id - 8) & (slot < lengths)
    train_mask = jnp.where(train_mask, 1.0, 0.0).astype(jnp.bfloat16)
    query_mask = jnp.where(query_mask, 1.0, 0.0).astype(jnp.bfloat16)
    masks = jnp.concatenate([train_mask, query_mask, train_mask, query_mask], axis=1)
    real_lengths = lengths[:, :1].astype(jnp.float32)

    got_outer[me_t] = acc[pl.ds(0, outer_rows), :]
    got_inner[me_t] = acc[pl.ds(pl.multiple_of(outer_rows + lax.rem(me_t, 2) * both_rows, 8), both_rows), :]
    for copy in outer_copies + inner_copies:
        copy.wait_recv()
    outer_sum, inner_sum = got_outer[0], got_inner[0]
    for t in range(1, tensor):
        outer_sum, inner_sum = outer_sum + got_outer[t], inner_sum + got_inner[t]

    outer_sum = jnp.concatenate([outer_sum[:rank_out], unpack(outer_sum[rank_out:], rank_out, rows_q)], axis=1)
    products = []
    for h in range(half):
        block = inner_sum[h * inner_rows : (h + 1) * inner_rows]
        block = jnp.concatenate([block[:share], unpack(block[share:], share, rows_q)], axis=1)
        products += [block[i : i + 1, :] * outer_sum for i in range(share)]
    products = jnp.concatenate(products, axis=0)
    high = products.astype(jnp.bfloat16)
    low = (products - high.astype(jnp.float32)).astype(jnp.bfloat16)
    summed = lax.dot_general(
        masks, jnp.concatenate([high, low], axis=1), contract, preferred_element_type=jnp.float32
    )
    mine = (summed / real_lengths).astype(jnp.bfloat16)
    grads[me_d] = mine

    grad_copies = []
    for k, peer in enumerate(peers_d):
        copy = pltpu.make_async_remote_copy(
            src_ref=grads.at[me_d],
            dst_ref=grads.at[me_d],
            send_sem=send_grads.at[k],
            recv_sem=recv_grads.at[k],
            device_id={"dp": peer},
            device_id_type=MESH,
        )
        copy.start()
        grad_copies.append(copy)
    out_grads[...] = mine
    for copy in grad_copies:
        copy.wait_recv()

    everyone = grads[...].reshape(dp * ROWS, mine.shape[1])
    gram = lax.dot_general(everyone, everyone, contract, preferred_element_type=jnp.float32)
    gram = jnp.concatenate([gram[d * ROWS : d * ROWS + 8, :] for d in range(dp)], axis=0)
    mine_at = lax.rem(me_t, 2)
    grams[mine_at, :, pl.ds(0, dp * ROWS)] = gram
    gram_copy = pltpu.make_async_remote_copy(
        src_ref=grams.at[mine_at],
        dst_ref=grams.at[mine_at],
        send_sem=send_gram.at[0],
        recv_sem=recv_gram.at[0],
        device_id={"tensor": me_t + 1 - 2 * mine_at},
        device_id_type=MESH,
    )
    gram_copy.start()
    gram_copy.wait_recv()
    whole = grams[0][:, : dp * ROWS] + grams[1][:, : dp * ROWS]

    out_gram[...] = whole
    for copy in outer_copies + inner_copies + grad_copies + [gram_copy]:
        copy.wait_send()


def solve_kernel(dp, query_count, mine, gram, damp, out_train, out_query, out_scores, train, query, solved, scores, sems):
    me_d = lax.axis_index("dp")
    features = train.shape[1]
    at = pl.ds(pl.multiple_of(lax.axis_index("tensor") // 2 * features, features), features)
    train[...] = mine[pl.ds(0, 8), at]
    query[...] = mine[pl.ds(8, query_count), at]
    stores = [
        pltpu.make_async_copy(train, out_train, sems.at[0]),
        pltpu.make_async_copy(query, out_query, sems.at[1]),
        pltpu.make_async_copy(scores, out_scores, sems.at[2]),
    ]
    stores[0].start()
    stores[1].start()
    whole = gram[...]
    total = dp * 8
    row = lax.broadcasted_iota(jnp.int32, whole.shape, 0)
    lane = lax.broadcasted_iota(jnp.int32, whole.shape, 1)
    diagonal = lane == (row // 8) * ROWS + row % 8
    trace = jnp.sum(jnp.where(diagonal, whole, 0.0), axis=(0, 1), keepdims=True)
    scale_code = damp[0:1, 0:1].astype(jnp.float32) / 10.0
    system = whole / trace
    system = jnp.where(diagonal, system + scale_code / total, system)
    columns = [(e // 8) * ROWS + e % 8 for e in range(total)]
    solved[...] = eliminate(system, columns)
    picked = solved[pl.ds(pl.multiple_of(me_d * 8, 8), 8), :] * total
    for d in range(dp):
        scores[:, d * query_count : (d + 1) * query_count] = picked[
            :, d * ROWS + 8 : d * ROWS + 8 + query_count
        ]

    stores[2].start()
    for store in stores:
        store.wait()


def fused_call(x_train, gout_train, x_query, gout_query, proj_in, proj_out, train_lengths, query_lengths, damping):
    tensor, dp = lax.axis_size("tensor"), lax.axis_size("dp")
    query_count = query_lengths.shape[0]
    rank_in, rank_out = proj_in.shape[1], proj_out.shape[1]
    depth_in, depth_out = proj_in.shape[0], proj_out.shape[0]
    tokens = x_train.shape[0] + x_query.shape[0]
    share = rank_in // tensor
    features = share * rank_out
    half = tensor // 2
    outer_rows = rank_out + packed_rows(rank_out, x_query.shape[0])
    inner_rows = share + packed_rows(share, x_query.shape[0])
    anywhere = pl.BlockSpec(memory_space=pltpu.HBM)
    vmem = pl.BlockSpec(memory_space=pltpu.VMEM)
    dma = pltpu.SemaphoreType.DMA
    hbm = lambda array: pltpu.with_memory_space_constraint(array, pltpu.HBM)
    mine, gram = pl.pallas_call(
        functools.partial(fused_kernel, tensor, dp, query_count),
        out_shape=(
            jax.ShapeDtypeStruct((ROWS, half * features), jnp.bfloat16),
            jax.ShapeDtypeStruct((dp * 8, dp * ROWS), jnp.float32),
        ),
        in_specs=[anywhere] * 8,
        out_specs=(vmem, vmem),
        scratch_shapes=[
            pltpu.VMEM((tokens, depth_in), jnp.bfloat16),
            pltpu.VMEM((tokens, depth_out), jnp.bfloat16),
            pltpu.VMEM((rank_in, depth_in), jnp.bfloat16),
            pltpu.VMEM((rank_out, depth_out), jnp.bfloat16),
            pltpu.SMEM(train_lengths.shape, jnp.int32),
            pltpu.SMEM(query_lengths.shape, jnp.int32),
            pltpu.VMEM((outer_rows + tensor * inner_rows, 128), jnp.float32),
            pltpu.VMEM((tensor, half * inner_rows, 128), jnp.float32),
            pltpu.VMEM((tensor, outer_rows, 128), jnp.float32),
            pltpu.VMEM((dp, ROWS, half * features), jnp.bfloat16),
            pltpu.VMEM((2, dp * 8, 128), jnp.float32),
            dma((3 + 3 * CHUNKS,)),
            dma((2,)),
            dma((tensor - 1,)),
            dma((tensor - 1,)),
            dma((tensor - 1,)),
            dma((tensor - 1,)),
            dma((dp - 1,)),
            dma((dp - 1,)),
            dma((1,)),
            dma((1,)),
        ],
        compiler_params=pltpu.CompilerParams(
            collective_id=0, has_side_effects=True, vmem_limit_bytes=16 << 20
        ),
        name="fused_grams",
    )(
        hbm(x_train),
        hbm(gout_train),
        hbm(x_query),
        hbm(gout_query),
        hbm(proj_in.T),
        hbm(proj_out.T),
        hbm(train_lengths),
        hbm(query_lengths),
    )
    return pl.pallas_call(
        functools.partial(solve_kernel, dp, query_count),
        out_shape=(
            jax.ShapeDtypeStruct((8, features), jnp.bfloat16),
            jax.ShapeDtypeStruct((query_count, features), jnp.bfloat16),
            jax.ShapeDtypeStruct((8, dp * query_count), jnp.float32),
        ),
        in_specs=[vmem, vmem, vmem],
        out_specs=[anywhere] * 3,
        scratch_shapes=[
            pltpu.VMEM((8, features), jnp.bfloat16),
            pltpu.VMEM((query_count, features), jnp.bfloat16),
            pltpu.VMEM((dp * 8, dp * ROWS), jnp.float32),
            pltpu.VMEM((8, dp * query_count), jnp.float32),
            dma((3,)),
        ],
        name="solve_scores",
    )(
        pltpu.with_memory_space_constraint(mine, pltpu.VMEM),
        pltpu.with_memory_space_constraint(gram, pltpu.VMEM),
        pltpu.with_memory_space_constraint(jnp.broadcast_to(damping, (8, 128)), pltpu.VMEM),
    )


def shards(
    x_train,
    gout_train,
    x_query,
    gout_query,
    proj_in,
    proj_out,
    train_lengths,
    query_lengths,
    damping,
):
    local_train = train_lengths.shape[0]
    total_train = local_train * lax.axis_size("dp")
    if fits_fused(x_train, x_query, proj_in, proj_out, train_lengths, query_lengths):
        return fused_call(
            x_train, gout_train, x_query, gout_query, proj_in, proj_out, train_lengths, query_lengths, damping
        )
    first = lax.axis_index("dp") * local_train
    scale_code = damping[0].astype(jnp.float32) / 10.0
    train_inner = jnp.dot(x_train, proj_in, preferred_element_type=jnp.float32)
    query_inner = jnp.dot(x_query, proj_in, preferred_element_type=jnp.float32)
    train_outer = jnp.dot(gout_train, proj_out, preferred_element_type=jnp.float32)
    query_outer = jnp.dot(gout_query, proj_out, preferred_element_type=jnp.float32)
    summed = lax.psum((train_inner, query_inner, train_outer, query_outer), "tensor")
    train_full = weighted_grads(summed[0], summed[2], train_lengths)
    query_full = weighted_grads(summed[1], summed[3], query_lengths)
    share = train_full.shape[1] // lax.axis_size("tensor")
    offset = lax.axis_index("tensor") * share
    train_grads = lax.dynamic_slice_in_dim(train_full, offset, share, 1)
    query_grads = lax.dynamic_slice_in_dim(query_full, offset, share, 1)
    all_train, all_query = (
        lax.all_gather(train_full, "dp", axis=0, tiled=True),
        lax.all_gather(query_full, "dp", axis=0, tiled=True),
    )
    kernel = jnp.dot(all_train, all_train.T, preferred_element_type=jnp.float32)
    cross = jnp.dot(all_train, all_query.T, preferred_element_type=jnp.float32)
    scores = kernel_scores(kernel, cross, scale_code, total_train, first, local_train)
    return (train_grads, query_grads, scores)


def solution(mesh):
    placed = (
        P(("grp", "dp"), "tensor"),
        P(("grp", "dp"), "tensor"),
        P(("grp", "dp"), "tensor"),
        P(("grp", "dp"), "tensor"),
        P("tensor", None),
        P("tensor", None),
        P(("grp", "dp")),
        P(("grp", "dp")),
        P(),
    )
    return jax.shard_map(
        shards,
        mesh=mesh,
        in_specs=placed,
        out_specs=(P(("grp", "dp"), "tensor"), P(("grp", "dp"), "tensor"), P(("grp", "dp"), None)),
        check_vma=False,
    )
```

```python
import functools

import jax
import jax.numpy as jnp
from jax import lax
from jax.experimental import pallas as pl
from jax.experimental.pallas import tpu as pltpu
from jax.sharding import PartitionSpec as P


def weighted_grads(inner, outer, lengths):
    count = lengths.shape[0]
    slots = inner.shape[0] // count
    inner = inner.reshape(count, slots, inner.shape[1])
    outer = outer.reshape(count, slots, outer.shape[1])
    valid = (lax.broadcasted_iota(jnp.int32, (count, slots), 1) < lengths[:, None]).astype(
        jnp.float32
    )
    weight = valid / lengths[:, None].astype(jnp.float32)
    summed = jnp.einsum(
        "eti,eto->eio", inner * weight[:, :, None], outer, precision=lax.Precision.HIGHEST
    )
    return summed.reshape(count, -1).astype(jnp.bfloat16)


def kernel_scores(kernel, cross, scale_code, total_train, first, local_train):
    trace = jnp.trace(kernel)
    ridge = scale_code * trace / total_train
    system = kernel + ridge * jnp.eye(total_train, dtype=jnp.float32)
    factor = jnp.linalg.cholesky(system)
    solved = jax.scipy.linalg.cho_solve((factor, True), cross)
    picked = lax.dynamic_slice_in_dim(solved, first, local_train, 0)
    return picked * total_train


MESH = pl.DeviceIdType.MESH
CHUNKS = 4
ROWS = 16


def fits_fused(x_train, x_query, proj_in, proj_out, train_lengths, query_lengths):
    train_count, query_count = train_lengths.shape[0], query_lengths.shape[0]
    tensor, dp = lax.axis_size("tensor"), lax.axis_size("dp")
    return (
        tensor > 1
        and tensor % 2 == 0
        and dp > 1
        and train_count == 8
        and query_count <= 8
        and x_train.shape[0] == 128
        and x_query.shape[0] <= 128
        and 128 % x_query.shape[0] == 0
        and x_query.shape[0] // query_count == 16
        and proj_in.shape[0] % (128 * CHUNKS) == 0
        and proj_in.shape[1] % (8 * tensor) == 0
        and proj_out.shape[1] % 8 == 0
        and dp * ROWS <= 128
    )


def eliminate(system, columns):
    shape = system.shape
    row_id = lax.broadcasted_iota(jnp.int32, shape, 0)

    def inverse_of(first, second, k):
        a, b = first[k : k + 1], second[k : k + 1]
        c, d = first[k + 1 : k + 2], second[k + 1 : k + 2]
        factor = 1.0 / (a * d - b * c)
        a, b, c, d = a * factor, b * factor, c * factor, d * factor
        return lambda top, bottom: (d * top - b * bottom, a * bottom - c * top)

    def cleared(values, first, second, top, bottom, k):
        rest = values - first * top - second * bottom
        return jnp.where(row_id == k, top, jnp.where(row_id == k + 1, bottom, rest))

    for k in range(0, len(columns), 4):
        c0, c1, c2, c3 = [jnp.broadcast_to(system[:, c : c + 1], shape) for c in columns[k : k + 4]]
        apply = inverse_of(c0, c1, k)
        top, bottom = apply(system[k : k + 1], system[k + 1 : k + 2])
        c2 = cleared(c2, c0, c1, *apply(c2[k : k + 1], c2[k + 1 : k + 2]), k)
        c3 = cleared(c3, c0, c1, *apply(c3[k : k + 1], c3[k + 1 : k + 2]), k)
        system = cleared(system, c0, c1, top, bottom, k)
        apply = inverse_of(c2, c3, k + 2)
        top, bottom = apply(system[k + 2 : k + 3], system[k + 3 : k + 4])
        system = cleared(system, c2, c3, top, bottom, k + 2)
    return system


def packed_rows(count, lanes):
    groups = count // 8
    return -(-groups // (128 // lanes)) * 8


def pack(values):
    count, lanes = values.shape
    beside = 128 // lanes
    groups = [values[g : g + 8] for g in range(0, count, 8)]
    groups += [jnp.zeros_like(groups[0])] * (-len(groups) % beside)
    lines = [jnp.concatenate(groups[g : g + beside], axis=1) for g in range(0, len(groups), beside)]
    return jnp.concatenate(lines, axis=0) if len(lines) > 1 else lines[0]


def unpack(packed, count, lanes):
    beside = 128 // lanes
    groups = []
    for g in range(count // 8):
        line, place = packed[g // beside * 8 : g // beside * 8 + 8], g % beside
        groups.append(pltpu.roll(line, 128 - place * lanes, 1) if place else line)
    return jnp.concatenate(groups, axis=0)


def partners(me, size):
    if size == 4:
        return [3 - me, lax.rem(me + 2, 4), me + 1 - 2 * lax.rem(me, 2)]
    return [lax.rem(me + k, size) for k in range(1, size)]


def fused_kernel(
    tensor,
    dp,
    query_count,
    xt,
    gt,
    xq,
    gq,
    pin,
    pout,
    tlen,
    qlen,
    out_grads,
    out_gram,
    xv,
    gv,
    piv,
    pov,
    tls,
    qls,
    acc,
    got_inner,
    got_outer,
    grads,
    grams,
    load_sem,
    small_sem,
    send_outer,
    recv_outer,
    send_inner,
    recv_inner,
    send_grads,
    recv_grads,
    send_gram,
    recv_gram,
):
    me_t, me_d = lax.axis_index("tensor"), lax.axis_index("dp")
    peers_t, peers_d = partners(me_t, tensor), partners(me_d, dp)
    barrier = pltpu.get_barrier_semaphore()
    for peer in peers_t:
        pl.semaphore_signal(barrier, inc=1, device_id={"tensor": peer}, device_id_type=MESH)
    for peer in peers_d:
        pl.semaphore_signal(barrier, inc=1, device_id={"dp": peer}, device_id_type=MESH)

    rows_t, rows_q = xt.shape[0], xq.shape[0]
    rank_in, rank_out = pin.shape[0], pout.shape[0]
    share = rank_in // tensor
    width = pin.shape[1] // CHUNKS
    packed_out, packed_in = packed_rows(rank_out, rows_q), packed_rows(share, rows_q)

    loads = [
        pltpu.make_async_copy(gt, gv.at[pl.ds(0, rows_t), :], load_sem.at[0]),
        pltpu.make_async_copy(gq, gv.at[pl.ds(rows_t, rows_q), :], load_sem.at[1]),
        pltpu.make_async_copy(pout, pov, load_sem.at[2]),
    ]
    chunk_loads = []
    for chunk in range(CHUNKS):
        at = pl.ds(chunk * width, width)
        base = 3 + 3 * chunk
        chunk_loads.append(
            [
                pltpu.make_async_copy(xt.at[:, at], xv.at[pl.ds(0, rows_t), at], load_sem.at[base]),
                pltpu.make_async_copy(xq.at[:, at], xv.at[pl.ds(rows_t, rows_q), at], load_sem.at[base + 1]),
                pltpu.make_async_copy(pin.at[:, at], piv.at[:, at], load_sem.at[base + 2]),
            ]
        )
    small = [
        pltpu.make_async_copy(tlen, tls, small_sem.at[0]),
        pltpu.make_async_copy(qlen, qls, small_sem.at[1]),
    ]
    for copy in loads:
        copy.start()
    for group in chunk_loads:
        for copy in group:
            copy.start()
    for copy in small:
        copy.start()

    contract = (((1,), (1,)), ((), ()))

    for copy in loads:
        copy.wait()
    outer = lax.dot_general(pov[...], gv[...], contract, preferred_element_type=jnp.float32)
    outer_rows = rank_out + packed_out
    acc[pl.ds(0, rank_out), :] = outer[:, :rows_t]
    acc[pl.ds(rank_out, packed_out), :] = pack(outer[:, rows_t:])

    inner = None
    for chunk in range(CHUNKS):
        for copy in chunk_loads[chunk]:
            copy.wait()
        at = pl.ds(chunk * width, width)
        part = lax.dot_general(piv[:, at], xv[:, at], contract, preferred_element_type=jnp.float32)
        inner = part if inner is None else inner + part
    inner_rows = share + packed_in
    half = tensor // 2
    both_rows = half * inner_rows
    for t in range(tensor):
        base = outer_rows + (t % 2 * half + t // 2) * inner_rows
        acc[pl.ds(base, share), :] = inner[t * share : (t + 1) * share, :rows_t]
        acc[pl.ds(base + share, packed_in), :] = pack(inner[t * share : (t + 1) * share, rows_t:])

    pl.semaphore_wait(barrier, tensor - 1 + dp - 1)
    outer_copies, inner_copies = [], []
    for k, peer in enumerate(peers_t):
        copy = pltpu.make_async_remote_copy(
            src_ref=acc.at[pl.ds(0, outer_rows), :],
            dst_ref=got_outer.at[me_t],
            send_sem=send_outer.at[k],
            recv_sem=recv_outer.at[k],
            device_id={"tensor": peer},
            device_id_type=MESH,
        )
        copy.start()
        outer_copies.append(copy)
        copy = pltpu.make_async_remote_copy(
            src_ref=acc.at[pl.ds(pl.multiple_of(outer_rows + lax.rem(peer, 2) * both_rows, 8), both_rows), :],
            dst_ref=got_inner.at[me_t],
            send_sem=send_inner.at[k],
            recv_sem=recv_inner.at[k],
            device_id={"tensor": peer},
            device_id_type=MESH,
        )
        copy.start()
        inner_copies.append(copy)

    for copy in small:
        copy.wait()
    row_id = lax.broadcasted_iota(jnp.int32, (ROWS, 128), 0)
    lane_id = lax.broadcasted_iota(jnp.int32, (ROWS, 128), 1)
    lengths = jnp.ones((ROWS, 128), jnp.int32)
    for e in range(8):
        lengths = jnp.where(row_id == e, tls[e], lengths)
    for e in range(query_count):
        lengths = jnp.where(row_id == 8 + e, qls[e], lengths)
    slot, example = lane_id % 16, lane_id // 16
    train_mask = (row_id < 8) & (example == row_id) & (slot < lengths)
    query_mask = (row_id >= 8) & (row_id < 8 + query_count) & (example == row_id - 8) & (slot < lengths)
    train_mask = jnp.where(train_mask, 1.0, 0.0).astype(jnp.bfloat16)
    query_mask = jnp.where(query_mask, 1.0, 0.0).astype(jnp.bfloat16)
    masks = jnp.concatenate([train_mask, query_mask, train_mask, query_mask], axis=1)
    real_lengths = lengths[:, :1].astype(jnp.float32)

    got_outer[me_t] = acc[pl.ds(0, outer_rows), :]
    got_inner[me_t] = acc[pl.ds(pl.multiple_of(outer_rows + lax.rem(me_t, 2) * both_rows, 8), both_rows), :]
    for copy in outer_copies + inner_copies:
        copy.wait_recv()
    outer_sum, inner_sum = got_outer[0], got_inner[0]
    for t in range(1, tensor):
        outer_sum, inner_sum = outer_sum + got_outer[t], inner_sum + got_inner[t]

    outer_sum = jnp.concatenate([outer_sum[:rank_out], unpack(outer_sum[rank_out:], rank_out, rows_q)], axis=1)
    products = []
    for h in range(half):
        block = inner_sum[h * inner_rows : (h + 1) * inner_rows]
        block = jnp.concatenate([block[:share], unpack(block[share:], share, rows_q)], axis=1)
        products += [block[i : i + 1, :] * outer_sum for i in range(share)]
    products = jnp.concatenate(products, axis=0)
    high = products.astype(jnp.bfloat16)
    low = (products - high.astype(jnp.float32)).astype(jnp.bfloat16)
    summed = lax.dot_general(
        masks, jnp.concatenate([high, low], axis=1), contract, preferred_element_type=jnp.float32
    )
    mine = (summed / real_lengths).astype(jnp.bfloat16)
    grads[me_d] = mine

    grad_copies = []
    for k, peer in enumerate(peers_d):
        copy = pltpu.make_async_remote_copy(
            src_ref=grads.at[me_d],
            dst_ref=grads.at[me_d],
            send_sem=send_grads.at[k],
            recv_sem=recv_grads.at[k],
            device_id={"dp": peer},
            device_id_type=MESH,
        )
        copy.start()
        grad_copies.append(copy)
    out_grads[...] = mine
    for copy in grad_copies:
        copy.wait_recv()

    everyone = grads[...].reshape(dp * ROWS, mine.shape[1])
    gram = lax.dot_general(everyone, everyone, contract, preferred_element_type=jnp.float32)
    gram = jnp.concatenate([gram[d * ROWS : d * ROWS + 8, :] for d in range(dp)], axis=0)
    mine_at = lax.rem(me_t, 2)
    grams[mine_at, :, pl.ds(0, dp * ROWS)] = gram
    gram_copy = pltpu.make_async_remote_copy(
        src_ref=grams.at[mine_at],
        dst_ref=grams.at[mine_at],
        send_sem=send_gram.at[0],
        recv_sem=recv_gram.at[0],
        device_id={"tensor": me_t + 1 - 2 * mine_at},
        device_id_type=MESH,
    )
    gram_copy.start()
    gram_copy.wait_recv()
    whole = grams[0][:, : dp * ROWS] + grams[1][:, : dp * ROWS]

    out_gram[...] = whole
    for copy in outer_copies + inner_copies + grad_copies + [gram_copy]:
        copy.wait_send()


def solve_kernel(dp, query_count, mine, gram, damp, out_train, out_query, out_scores, train, query, solved, scores, sems):
    me_d = lax.axis_index("dp")
    features = train.shape[1]
    at = pl.ds(pl.multiple_of(lax.axis_index("tensor") // 2 * features, features), features)
    train[...] = mine[pl.ds(0, 8), at]
    query[...] = mine[pl.ds(8, query_count), at]
    stores = [
        pltpu.make_async_copy(train, out_train, sems.at[0]),
        pltpu.make_async_copy(query, out_query, sems.at[1]),
        pltpu.make_async_copy(scores, out_scores, sems.at[2]),
    ]
    stores[0].start()
    stores[1].start()
    whole = gram[...]
    total = dp * 8
    row = lax.broadcasted_iota(jnp.int32, whole.shape, 0)
    lane = lax.broadcasted_iota(jnp.int32, whole.shape, 1)
    diagonal = lane == (row // 8) * ROWS + row % 8
    trace = jnp.sum(jnp.where(diagonal, whole, 0.0), axis=(0, 1), keepdims=True)
    scale_code = damp[0:1, 0:1].astype(jnp.float32) / 10.0
    system = whole / trace
    system = jnp.where(diagonal, system + scale_code / total, system)
    columns = [(e // 8) * ROWS + e % 8 for e in range(total)]
    solved[...] = eliminate(system, columns)
    picked = solved[pl.ds(pl.multiple_of(me_d * 8, 8), 8), :] * total
    for d in range(dp):
        scores[:, d * query_count : (d + 1) * query_count] = picked[
            :, d * ROWS + 8 : d * ROWS + 8 + query_count
        ]

    stores[2].start()
    for store in stores:
        store.wait()


def fused_call(x_train, gout_train, x_query, gout_query, proj_in, proj_out, train_lengths, query_lengths, damping):
    tensor, dp = lax.axis_size("tensor"), lax.axis_size("dp")
    query_count = query_lengths.shape[0]
    rank_in, rank_out = proj_in.shape[1], proj_out.shape[1]
    depth_in, depth_out = proj_in.shape[0], proj_out.shape[0]
    tokens = x_train.shape[0] + x_query.shape[0]
    share = rank_in // tensor
    features = share * rank_out
    half = tensor // 2
    outer_rows = rank_out + packed_rows(rank_out, x_query.shape[0])
    inner_rows = share + packed_rows(share, x_query.shape[0])
    anywhere = pl.BlockSpec(memory_space=pltpu.HBM)
    vmem = pl.BlockSpec(memory_space=pltpu.VMEM)
    dma = pltpu.SemaphoreType.DMA
    hbm = lambda array: pltpu.with_memory_space_constraint(array, pltpu.HBM)
    mine, gram = pl.pallas_call(
        functools.partial(fused_kernel, tensor, dp, query_count),
        out_shape=(
            jax.ShapeDtypeStruct((ROWS, half * features), jnp.bfloat16),
            jax.ShapeDtypeStruct((dp * 8, dp * ROWS), jnp.float32),
        ),
        in_specs=[anywhere] * 8,
        out_specs=(vmem, vmem),
        scratch_shapes=[
            pltpu.VMEM((tokens, depth_in), jnp.bfloat16),
            pltpu.VMEM((tokens, depth_out), jnp.bfloat16),
            pltpu.VMEM((rank_in, depth_in), jnp.bfloat16),
            pltpu.VMEM((rank_out, depth_out), jnp.bfloat16),
            pltpu.SMEM(train_lengths.shape, jnp.int32),
            pltpu.SMEM(query_lengths.shape, jnp.int32),
            pltpu.VMEM((outer_rows + tensor * inner_rows, 128), jnp.float32),
            pltpu.VMEM((tensor, half * inner_rows, 128), jnp.float32),
            pltpu.VMEM((tensor, outer_rows, 128), jnp.float32),
            pltpu.VMEM((dp, ROWS, half * features), jnp.bfloat16),
            pltpu.VMEM((2, dp * 8, 128), jnp.float32),
            dma((3 + 3 * CHUNKS,)),
            dma((2,)),
            dma((tensor - 1,)),
            dma((tensor - 1,)),
            dma((tensor - 1,)),
            dma((tensor - 1,)),
            dma((dp - 1,)),
            dma((dp - 1,)),
            dma((1,)),
            dma((1,)),
        ],
        compiler_params=pltpu.CompilerParams(
            collective_id=0, has_side_effects=True, vmem_limit_bytes=16 << 20
        ),
        name="fused_grams",
    )(
        hbm(x_train),
        hbm(gout_train),
        hbm(x_query),
        hbm(gout_query),
        hbm(proj_in.T),
        hbm(proj_out.T),
        hbm(train_lengths),
        hbm(query_lengths),
    )
    return pl.pallas_call(
        functools.partial(solve_kernel, dp, query_count),
        out_shape=(
            jax.ShapeDtypeStruct((8, features), jnp.bfloat16),
            jax.ShapeDtypeStruct((query_count, features), jnp.bfloat16),
            jax.ShapeDtypeStruct((8, dp * query_count), jnp.float32),
        ),
        in_specs=[vmem, vmem, vmem],
        out_specs=[anywhere] * 3,
        scratch_shapes=[
            pltpu.VMEM((8, features), jnp.bfloat16),
            pltpu.VMEM((query_count, features), jnp.bfloat16),
            pltpu.VMEM((dp * 8, dp * ROWS), jnp.float32),
            pltpu.VMEM((8, dp * query_count), jnp.float32),
            dma((3,)),
        ],
        name="solve_scores",
    )(
        pltpu.with_memory_space_constraint(mine, pltpu.VMEM),
        pltpu.with_memory_space_constraint(gram, pltpu.VMEM),
        pltpu.with_memory_space_constraint(jnp.broadcast_to(damping, (8, 128)), pltpu.VMEM),
    )


def shards(
    x_train,
    gout_train,
    x_query,
    gout_query,
    proj_in,
    proj_out,
    train_lengths,
    query_lengths,
    damping,
):
    local_train = train_lengths.shape[0]
    total_train = local_train * lax.axis_size("dp")
    if fits_fused(x_train, x_query, proj_in, proj_out, train_lengths, query_lengths):
        return fused_call(
            x_train, gout_train, x_query, gout_query, proj_in, proj_out, train_lengths, query_lengths, damping
        )
    first = lax.axis_index("dp") * local_train
    scale_code = damping[0].astype(jnp.float32) / 10.0
    train_inner = jnp.dot(x_train, proj_in, preferred_element_type=jnp.float32)
    query_inner = jnp.dot(x_query, proj_in, preferred_element_type=jnp.float32)
    train_outer = jnp.dot(gout_train, proj_out, preferred_element_type=jnp.float32)
    query_outer = jnp.dot(gout_query, proj_out, preferred_element_type=jnp.float32)
    summed = lax.psum((train_inner, query_inner, train_outer, query_outer), "tensor")
    train_full = weighted_grads(summed[0], summed[2], train_lengths)
    query_full = weighted_grads(summed[1], summed[3], query_lengths)
    share = train_full.shape[1] // lax.axis_size("tensor")
    offset = lax.axis_index("tensor") * share
    train_grads = lax.dynamic_slice_in_dim(train_full, offset, share, 1)
    query_grads = lax.dynamic_slice_in_dim(query_full, offset, share, 1)
    all_train, all_query = (
        lax.all_gather(train_full, "dp", axis=0, tiled=True),
        lax.all_gather(query_full, "dp", axis=0, tiled=True),
    )
    kernel = jnp.dot(all_train, all_train.T, preferred_element_type=jnp.float32)
    cross = jnp.dot(all_train, all_query.T, preferred_element_type=jnp.float32)
    scores = kernel_scores(kernel, cross, scale_code, total_train, first, local_train)
    return (train_grads, query_grads, scores)


def solution(mesh):
    placed = (
        P(("grp", "dp"), "tensor"),
        P(("grp", "dp"), "tensor"),
        P(("grp", "dp"), "tensor"),
        P(("grp", "dp"), "tensor"),
        P("tensor", None),
        P("tensor", None),
        P(("grp", "dp")),
        P(("grp", "dp")),
        P(),
    )
    return jax.shard_map(
        shards,
        mesh=mesh,
        in_specs=placed,
        out_specs=(P(("grp", "dp"), "tensor"), P(("grp", "dp"), "tensor"), P(("grp", "dp"), None)),
        check_vma=False,
    )
```
